32 devices in a mesh: grp: 4 (over x, core), blk: 8 (over z, y).
Axes of the slice: x: 2, y: 2, z: 4, core: 2. Of those that a mesh axis runs over, the one named last changes fastest.
Arguments:
- raw: bfloat16 [4, 4, 1024, 256], P('grp', None, 'blk'), may hold values from -6 to 6
- raw_kin: bfloat16 [4, 4, 4, 1024], P('grp', None, None, 'blk'), may hold values from -3.2 to 20, as said below
- reader: int32 [4, 1024], P('grp', 'blk'), may hold values from 0 to 3
- event_id: int32 [4, 1024], P('grp', 'blk'), may hold values from 0 to 7, never falling along the last dimension, each value on 1 to 512 neighbouring positions
- pre_gain: float32 [256], replicated, may hold values from 0.25 to 1.75
- w_query: bfloat16 [256, 256], replicated, may hold values from -2 to 2
- w_key: bfloat16 [256, 256], replicated, may hold values from -2 to 2
- w_value: bfloat16 [256, 256], replicated, may hold values from -0.375 to 0.375
- w_out: bfloat16 [256, 256], replicated, may hold values from -0.375 to 0.375
- post_gain: float32 [256], replicated, may hold values from 0.25 to 1.75
- pair_w1: float32 [4, 32], replicated, may hold values from -3 to 3
- pair_b1: float32 [32], replicated, may hold values from -4 to 4
- pair_w2: float32 [32, 8], replicated, may hold values from -1 to 1
Outputs:
- encoded: bfloat16 [4, 1024, 256], P('grp', 'blk')
The draws below stay inside these ranges and needn't reach their ends.
Inputs may be any that keep to these rules, and one draw needn't show every extreme that they name: `raw_kin`: rows are transverse momentum (positive), rapidity, azimuth and mass (positive). `event_id`: event numbers never fall along a group's slots; every event holds 1 to 512 slots and some event exactly 512.
All inputs are finite; a program needn't handle non-finite values.
Results may differ from the reference program's by a relative error of at most 0.0091.
Values may be sent and summed in bfloat16 or wider, within the bound.
No kernel may reach another device: no remote copies, remote signals or barrier semaphores. Data moves between devices by JAX's collectives and lax.ppermute only.
A program may use at most 64 MiB of HBM per device.

```python
import math
import jax
import jax.numpy as jnp
import numpy as np
from jax import lax

D = 256
HEADS = 8
PAIR_FEAT = 4
PAIR_HID = 32
EVENTS = 8
GROUPS = 4
SLOTS = 1024
MAXLEN = 512


def draw_raw_kin(key, part):
    shape = (GROUPS, GROUPS, SLOTS)
    trans_mom = jnp.exp(jax.random.uniform(jax.random.fold_in(key, 1), shape, jnp.float32, math.log(0.5), math.log(20.0)))
    rapidity = jax.random.uniform(jax.random.fold_in(key, 2), shape, jnp.float32, -2.5, 2.5)
    azimuth = jax.random.uniform(jax.random.fold_in(key, 3), shape, jnp.float32, -math.pi, math.pi)
    mass_val = jax.random.uniform(jax.random.fold_in(key, 4), shape, jnp.float32, 0.1, 1.0)
    return jnp.stack([trans_mom, rapidity, azimuth, mass_val], axis=2).astype(jnp.bfloat16)


def projection_parts(key):
    first = jax.random.normal(jax.random.fold_in(key, 12), (D, D), jnp.float32)
    second = jax.random.normal(jax.random.fold_in(key, 13), (D, D), jnp.float32)
    return (first, second)


def draw_w_query(key, part):
    first, second = projection_parts(key)
    value = first / math.sqrt(D)
    return jnp.clip(value, -2.0, 2.0).astype(jnp.bfloat16)


def draw_w_key(key, part):
    first, second = projection_parts(key)
    value = second / math.sqrt(D)
    return jnp.clip(value, -2.0, 2.0).astype(jnp.bfloat16)


def plant(array, own_key, low, largest):
    extent = array.shape
    place = [jax.random.randint(jax.random.fold_in(own_key, axis), (), 0, extent[axis]) for axis in range(len(extent))]
    array = array.at[tuple(place)].set(low)
    longest = extent.index(max(extent))
    place[longest] = (place[longest] + 1) % extent[longest]
    return array.at[tuple(place)].set(largest)


def steps_of(stream_key, extent, cuts, least, largest):
    level, own = 1.0, jax.random.fold_in(stream_key, 6)
    for axis_at, blocks in cuts:
        draws = jnp.exp(jax.random.uniform(jax.random.fold_in(own, axis_at), (blocks,), jnp.float32, least / len(cuts), largest / len(cuts)))
        level = level * jnp.repeat(draws, extent[axis_at] // blocks).reshape([-1 if axis == axis_at else 1 for axis in range(len(extent))])
    return level


def split_up(number_of, total, limit, lean):
    portions = [(1 << 20) // math.isqrt(rank ** lean) + 1 for rank in range(2, number_of + 1)]
    surplus, given = total - limit - (number_of - 1), [1] * (number_of - 1)
    while surplus > 0:
        movable = [i for i in range(number_of - 1) if given[i] < limit]
        mass, budget = sum([portions[i] for i in movable]), surplus
        for i in movable:
            addition = min(limit - given[i], max(1, budget * portions[i] // mass), surplus)
            given[i] = given[i] + addition
            surplus = surplus - addition
    return np.array([limit] + given)


def uneven(own_key, amount, total, reach, skew):
    if amount == 2:
        one = jax.random.randint(own_key, (), max(1, total - reach), min(reach, total - 1) + 1)
        return jnp.stack([one, total - one])
    sizes = jnp.asarray(split_up(amount, total, reach, skew), jnp.int32)
    couples = (amount - 1) // 2
    source_of, sink = sizes[1:1 + 2 * couples:2], sizes[2:2 + 2 * couples:2]
    margin = jnp.minimum(source_of - 1, reach - sink)
    shifted = jax.random.randint(jax.random.fold_in(own_key, 1), (couples,), 0, 1 << 20) % (margin + 1)
    sizes = sizes.at[1:1 + 2 * couples:2].set(source_of - shifted).at[2:2 + 2 * couples:2].set(sink + shifted)
    return sizes[jax.random.permutation(jax.random.fold_in(own_key, 2), amount)]


def normal_values(rng, extent, scale, bound, shards=(), kind=jnp.bfloat16):
    drawn = scale * jax.random.normal(rng, extent, jnp.float32)
    if shards:
        drawn = drawn * steps_of(rng, extent, shards, -0.22, 0.18)
    return jnp.clip(drawn, -bound, bound).astype(kind)


def setup_inputs(seed: int = 0) -> dict:
    streams_of = jax.random.split(jax.random.key(seed), 14)
    raw = normal_values(streams_of[0], (GROUPS, GROUPS, SLOTS, D), 1.0, 6.0, ((0, 4), (2, 8)))
    raw_kin = draw_raw_kin(jax.random.fold_in(streams_of[13], 71), 0)
    reader = plant(jax.random.randint(streams_of[2], (GROUPS, SLOTS), 0, GROUPS), jax.random.fold_in(streams_of[2], 1), 0, GROUPS - 1).astype(jnp.int32)
    event_id = jax.vmap(lambda own: jnp.searchsorted(jnp.cumsum(uneven(own, EVENTS, SLOTS, MAXLEN, 2)), jnp.arange(SLOTS), side="right"))(jax.random.split(streams_of[3], GROUPS)).reshape((GROUPS, SLOTS)).astype(jnp.int32)
    pre_gain = jnp.clip(1.0 + 0.15 * jax.random.normal(streams_of[4], (D,), jnp.float32), 0.25, 1.75)
    w_query = draw_w_query(jax.random.fold_in(streams_of[13], 71), 0)
    w_key = draw_w_key(jax.random.fold_in(streams_of[13], 71), 0)
    w_value = normal_values(streams_of[7], (D, D), D ** -0.5, 0.375)
    w_out = normal_values(streams_of[8], (D, D), D ** -0.5, 0.375)
    post_gain = jnp.clip(1.0 + 0.15 * jax.random.normal(streams_of[9], (D,), jnp.float32), 0.25, 1.75)
    pair_w1 = normal_values(streams_of[10], (PAIR_FEAT, PAIR_HID), PAIR_FEAT ** -0.5, 3.0, (), jnp.float32)
    pair_b1 = normal_values(streams_of[11], (PAIR_HID,), 1.0, 4.0, (), jnp.float32)
    pair_w2 = normal_values(streams_of[12], (PAIR_HID, HEADS), PAIR_HID ** -0.5, 1.0, (), jnp.float32)
    return dict(raw=raw, raw_kin=raw_kin, reader=reader, event_id=event_id, pre_gain=pre_gain, w_query=w_query, w_key=w_key, w_value=w_value, w_out=w_out, post_gain=post_gain, pair_w1=pair_w1, pair_b1=pair_b1, pair_w2=pair_w2)


exact_mode = lax.Precision.HIGHEST

def layer_norm(rows, gain):
    center = rows - lax.optimization_barrier(jnp.mean(rows, axis=-1, keepdims=True))
    spread = lax.optimization_barrier(jnp.mean(center * center, axis=-1, keepdims=True))
    return center * lax.rsqrt(spread + 1e-05) * gain

def particle_terms(kinematics):
    trans_mom = kinematics[0]
    rapidity = kinematics[1]
    azimuth = kinematics[2]
    mass_val = kinematics[3]
    trans_mass = jnp.sqrt(trans_mom * trans_mom + mass_val * mass_val)
    return (trans_mom, rapidity, jnp.cos(azimuth), jnp.sin(azimuth), trans_mass, mass_val * mass_val)

def pair_bias(query_terms, key_terms, pair_w1, pair_b1, pair_w2):
    q_mom, q_rap, q_cos, q_sin, q_trans, q_mass = [term[:, None] for term in query_terms]
    k_mom, k_rap, k_cos, k_sin, k_trans, k_mass = [term[None, :] for term in key_terms]
    rap_gap = q_rap - k_rap
    cos_gap = q_cos * k_cos + q_sin * k_sin
    dist_sq = rap_gap * rap_gap + 2.0 * (1.0 - cos_gap)
    low_mom = jnp.minimum(q_mom, k_mom)
    mass_sq = q_mass + k_mass + 2.0 * (q_trans * k_trans * jnp.cosh(rap_gap) - q_mom * k_mom * cos_gap)
    features = jnp.stack([jnp.log1p(dist_sq), jnp.log1p(low_mom * low_mom * dist_sq), low_mom / (q_mom + k_mom), jnp.log1p(mass_sq)])
    hidden = jax.nn.gelu(jnp.einsum('cqk,ch->hqk', features, pair_w1, precision=exact_mode) + pair_b1[:, None, None], approximate=True)
    return jnp.einsum('hqk,hn->nqk', hidden, pair_w2, precision=exact_mode)

def reference(raw, raw_kin, reader, event_id, pre_gain, w_query, w_key, w_value, w_out, post_gain, pair_w1, pair_b1, pair_w2):
    groups = raw.shape[0]
    slots = raw.shape[2]
    width = raw.shape[3]
    heads = pair_w2.shape[1]
    head_size = width // heads
    block_rows = min(256, slots)
    results = []
    for group in range(groups):
        picked = reader[group][None, :] == jnp.arange(groups, dtype=jnp.int32)[:, None]
        tokens = lax.optimization_barrier(jnp.sum(jnp.where(picked[:, :, None], raw[:, group].astype(jnp.float32), 0.0), axis=0))
        kinematics = lax.optimization_barrier(jnp.sum(jnp.where(picked[:, None, :], raw_kin[:, group].astype(jnp.float32), 0.0), axis=0))
        normed = layer_norm(tokens, pre_gain).astype(jnp.bfloat16)
        queries = jnp.dot(normed, w_query, preferred_element_type=jnp.float32).astype(jnp.bfloat16)
        keys = jnp.dot(normed, w_key, preferred_element_type=jnp.float32).astype(jnp.bfloat16)
        values = jnp.dot(normed, w_value, preferred_element_type=jnp.float32).astype(jnp.bfloat16)
        terms = particle_terms(kinematics)
        group_ids = event_id[group]
        key_heads = keys.astype(jnp.float32).T.reshape(heads, head_size, slots)
        value_heads = values.astype(jnp.float32).T.reshape(heads, head_size, slots)

        def query_block(index):
            start = (index * block_rows).astype(jnp.int32)
            block_q = lax.dynamic_slice_in_dim(queries, start, block_rows, 0).astype(jnp.float32)
            block_q = block_q.reshape(block_rows, heads, head_size)
            block_terms = tuple((lax.dynamic_slice_in_dim(term, start, block_rows, 0) for term in terms))
            block_ids = lax.dynamic_slice_in_dim(group_ids, start, block_rows, 0)
            scores = jnp.einsum('qhd,hdk->hqk', block_q, key_heads, precision=exact_mode) * head_size ** (-0.5)
            scores = scores + pair_bias(block_terms, terms, pair_w1, pair_b1, pair_w2)
            live = (block_ids[:, None] == group_ids[None, :])[None]
            top = lax.optimization_barrier(jnp.max(jnp.where(live, scores, jnp.float32(-1e+30)), axis=2))
            weights = jnp.where(live, jnp.exp(scores - top[:, :, None]), 0.0)
            totals = lax.optimization_barrier(jnp.sum(weights, axis=2))
            rounded = lax.optimization_barrier(weights.astype(jnp.bfloat16)).astype(jnp.float32)
            mixed = jnp.einsum('hqk,hdk->qhd', rounded, value_heads, precision=exact_mode)
            mixed = mixed / totals.T[:, :, None]
            return mixed.reshape(block_rows, width).astype(jnp.bfloat16)
        attended = lax.map(query_block, jnp.arange(slots // block_rows, dtype=jnp.int32)).reshape(slots, width)
        mixed_out = jnp.dot(attended, w_out, preferred_element_type=jnp.float32)
        results.append(layer_norm(mixed_out, post_gain).astype(jnp.bfloat16))
    return jnp.stack(results)
```

```python
import math

import jax
import jax.numpy as jnp
from jax import lax
from jax.experimental import pallas as pl
from jax.experimental.pallas import tpu as pltpu
from jax.sharding import PartitionSpec as P


F32 = jnp.float32
BF16 = jnp.bfloat16
EXTRA = 16
LANES = 128
TILE = 256
CHUNK = 128

SQ = math.sqrt(2.0 / math.pi)
GAMMA = (SQ * 0.044715) ** (1.0 / 3.0)
BETA = SQ / GAMMA
LOG2E = math.log2(math.e)


def layer_norm(rows, gain):
    center = rows - jnp.mean(rows, axis=-1, keepdims=True)
    spread = jnp.mean(center * center, axis=-1, keepdims=True)
    return center * lax.rsqrt(spread + 1e-05) * gain


def pack_kernel(place, raw_ref, kin_ref, *out_refs):
    rows = raw_ref.shape[1]
    groups = raw_ref.shape[0]
    width = raw_ref.shape[2]
    own = place[0]
    for step, out in enumerate(out_refs, start=1):
        target = lax.rem(own + step, groups)
        out[0:rows, :] = raw_ref[target]
        kin = kin_ref[target]
        if width > rows:
            kin = jnp.concatenate([kin, jnp.zeros((kin.shape[0], width - rows), BF16)], axis=1)
        out[rows : rows + EXTRA, :] = jnp.concatenate(
            [kin, jnp.zeros((EXTRA - kin.shape[0], width), BF16)], axis=0
        )


def select_kernel(place, raw_ref, kin_ref, reader_ref, ids_ref, gain_ref, *refs):
    got = refs[:-1]
    out = refs[-1]
    groups, rows, width = raw_ref.shape
    own = place[0]
    reader = reader_ref[...].astype(F32)
    by_lane = reader
    by_row = jnp.transpose(jnp.broadcast_to(reader, (LANES, rows)))
    by_row = jnp.concatenate([by_row] * (width // LANES), axis=1)
    tokens = jnp.where(by_row == own.astype(F32), raw_ref[own].astype(F32), 0.0)
    kin = jnp.where(by_lane == own.astype(F32), kin_ref[own].astype(F32), 0.0)
    for step, ref in enumerate(got, start=1):
        source = lax.rem(own + groups - step, groups).astype(F32)
        tokens = jnp.where(by_row == source, ref[0:rows, :].astype(F32), tokens)
        kin = jnp.where(by_lane == source, ref[rows : rows + 4, 0:rows].astype(F32), kin)
    out[0:rows, :] = layer_norm(tokens, gain_ref[...]).astype(BF16)
    block = jnp.concatenate([kin, ids_ref[...].astype(F32), jnp.zeros((EXTRA - 5, rows), F32)], axis=0)
    if width > rows:
        block = jnp.concatenate([block, jnp.zeros((EXTRA, width - rows), F32)], axis=1)
    out[rows : rows + EXTRA, :] = block.astype(BF16)


def split(value):
    high = value.astype(BF16)
    return high, (value - high.astype(F32)).astype(BF16)


def main_kernel(
    place,
    *refs,
    blocks,
    heads,
):
    got = refs[:blocks]
    (wq_ref, wk_ref, wv_ref, wo_ref, gain_ref, first_ref, second_ref, out_ref) = refs[blocks : blocks + 8]
    (kt_ref, v_ref, raw_ref, term_ref, qt_ref, qm_ref, s_ref, att_ref) = refs[blocks + 8 :]
    rows = got[0].shape[0] - EXTRA
    width = got[0].shape[1]
    head_size = width // heads
    per_tile = TILE // rows
    tiles = blocks * rows // TILE
    own = place[1]
    chunk = pl.program_id(0)

    @pl.when(chunk == 0)
    def prepare():
        for step, ref in enumerate(got):
            block = lax.rem(own + blocks - step, blocks)
            feats = ref[0:rows, :]
            kt = lax.dot_general(
                wk_ref[...], feats, (((0,), (1,)), ((), ())), preferred_element_type=F32
            )
            kt_ref[block] = kt.astype(BF16)
            v_ref[block] = jnp.dot(feats, wv_ref[...], preferred_element_type=F32).astype(BF16)
            extra = ref[rows : rows + EXTRA, 0:rows].astype(F32)
            for row in range(5):
                raw_ref[row, pl.ds(block, 1), :] = extra[row : row + 1, :]
        pt = raw_ref[0]
        rap = raw_ref[1]
        phi = raw_ref[2]
        mass = raw_ref[3]
        m2 = mass * mass
        mt = jnp.sqrt(pt * pt + m2)
        term_ref[0] = pt
        term_ref[1] = rap
        term_ref[2] = jnp.cos(phi)
        term_ref[3] = jnp.sin(phi)
        term_ref[4] = mt * jnp.exp(rap)
        term_ref[5] = mt * jnp.exp(-rap)
        term_ref[6] = m2
        term_ref[7] = raw_ref[4]

    start = pl.multiple_of(chunk * CHUNK, CHUNK)
    mine = jnp.concatenate([term_ref[t, pl.ds(own, 1), :] for t in range(8)], axis=0)
    if rows > CHUNK:
        mine = jnp.where(chunk == 0, mine[:, 0:CHUNK], mine[:, CHUNK : 2 * CHUNK])
    cols = jnp.transpose(jnp.concatenate([mine, jnp.zeros((LANES - 8, CHUNK), F32)], axis=0))
    for t in range(8):
        qt_ref[t] = jnp.broadcast_to(cols[:, t : t + 1], (CHUNK, LANES))
    feats = got[0][pl.ds(start, CHUNK), :]
    queries = jnp.dot(feats, wq_ref[...], preferred_element_type=F32).astype(BF16).astype(F32)
    lane_head = lax.broadcasted_iota(jnp.int32, (8, width), 1) // head_size
    for g in range(CHUNK // 8):
        piece = queries[8 * g : 8 * g + 8, :]
        qm_ref[g] = jnp.concatenate(
            [jnp.where(lane_head == h, piece, 0.0) for h in range(heads)], axis=0
        ).astype(BF16)

    first = first_ref[...]
    second = second_ref[...]
    scale = LOG2E * head_size ** (-0.5)

    def features(g, tile):
        parts = []
        lives = []
        at = pl.multiple_of(g * 8, 8)
        q = [qt_ref[t, pl.ds(at, 8), :] for t in range(8)]
        for piece in range(TILE // LANES):
            flat = piece * LANES
            block = tile * per_tile + flat // rows
            lane = flat % rows
            k = [term_ref[t, pl.ds(block, 1), lane : lane + LANES] for t in range(8)]
            gap = q[1] - k[1]
            cos_gap = q[2] * k[2] + q[3] * k[3]
            dist = gap * gap + 2.0 * (1.0 - cos_gap)
            low = jnp.minimum(q[0], k[0])
            pair_mass = q[6] + k[6] + (q[4] * k[5] + q[5] * k[4] - 2.0 * (q[0] * k[0]) * cos_gap)
            feats = [
                jnp.log(1.0 + dist),
                jnp.log(1.0 + low * low * dist),
                low / (q[0] + k[0]),
                jnp.log(1.0 + pair_mass),
            ]
            ab = jnp.concatenate(feats[0:2], axis=0)
            cd = jnp.concatenate(feats[2:4], axis=0)
            ab_hi, ab_lo = split(ab)
            cd_hi, cd_lo = split(cd)
            ones = jnp.ones((32, LANES), BF16)
            parts.append(jnp.concatenate([ab_hi, cd_hi, ab_lo, cd_lo, ab_hi, cd_hi, ones], axis=0))
            lives.append(q[7] == k[7])
        return jnp.concatenate(parts, axis=1), lives

    def one_tile(g, tile):
        feats, lives = features(g, tile)
        hidden = jnp.dot(first, feats, preferred_element_type=F32)
        act = hidden * (1.0 + jnp.tanh(hidden * (hidden * hidden + BETA)))
        bias2 = jnp.dot(second, act.astype(BF16), preferred_element_type=F32)
        bias = bias2[0 : 8 * heads, :] + bias2[8 * heads :, :]
        if per_tile > 1:
            keys = jnp.concatenate([kt_ref[tile * per_tile + i] for i in range(per_tile)], axis=1)
        else:
            keys = kt_ref[tile]
        scores = jnp.dot(qm_ref[g], keys, preferred_element_type=F32) * scale + bias
        for piece in range(TILE // LANES):
            live = jnp.concatenate([lives[piece]] * heads, axis=0) if False else lives[piece]
            lo = piece * LANES
            for h in range(heads):
                s_ref[tile, g, 8 * h : 8 * h + 8, lo : lo + LANES] = jnp.where(
                    live, scores[8 * h : 8 * h + 8, lo : lo + LANES], -1e30
                )

    groups = CHUNK // 8
    span = min(4, tiles)

    def pair_step(index, carry):
        g = index // (tiles // span)
        base = (index % (tiles // span)) * span
        for t in range(span):
            one_tile(g, base + t)
        return carry

    lax.fori_loop(0, groups * (tiles // span), pair_step, 0)

    row_head = lax.broadcasted_iota(jnp.int32, (8 * heads, width), 0) // 8
    col_head = lax.broadcasted_iota(jnp.int32, (8 * heads, width), 1) // head_size
    diag = row_head == col_head

    def attend(g, carry):
        top = s_ref[0, g]
        for t in range(1, tiles):
            top = jnp.maximum(top, s_ref[t, g])
        top = jnp.max(top, axis=1, keepdims=True)
        total = jnp.zeros((8 * heads, TILE), F32)
        accum = jnp.zeros((8 * heads, width), F32)
        for t in range(tiles):
            weights = jnp.exp2(s_ref[t, g] - top)
            total = total + weights
            if per_tile > 1:
                vals = jnp.concatenate([v_ref[t * per_tile + i] for i in range(per_tile)], axis=0)
            else:
                vals = v_ref[t]
            accum = accum + jnp.dot(weights.astype(BF16), vals, preferred_element_type=F32)
        total = jnp.sum(total, axis=1, keepdims=True)
        accum = jnp.where(diag, accum / total, 0.0)
        rows_out = accum[0:8, :]
        for h in range(1, heads):
            rows_out = rows_out + accum[8 * h : 8 * h + 8, :]
        att_ref[pl.ds(pl.multiple_of(g * 8, 8), 8), :] = rows_out
        return carry

    lax.fori_loop(0, groups, attend, 0)
    mixed = jnp.dot(att_ref[...].astype(BF16), wo_ref[...], preferred_element_type=F32)
    out_ref[...] = layer_norm(mixed, gain_ref[...]).astype(BF16)


def pair_weights(pair_w1, pair_b1, pair_w2):
    eye = jnp.eye(8, dtype=F32)
    hidden = pair_w1.shape[1]
    heads = pair_w2.shape[1]
    w1 = pair_w1.T * GAMMA
    w1_hi, w1_lo = split(w1)
    b1 = pair_b1 * GAMMA
    b_hi, b_lo = split(b1)
    b_lo2 = (b1 - b_hi.astype(F32) - b_lo.astype(F32)).astype(BF16)
    spread = lambda w: (w.astype(F32)[:, None, :, None] * eye[None, :, None, :]).reshape(hidden * 8, -1)
    column = lambda b: jnp.broadcast_to(b.astype(F32)[:, None], (hidden, 8)).reshape(hidden * 8, 1)
    first = jnp.concatenate(
        [
            spread(w1_hi),
            spread(w1_hi),
            spread(w1_lo),
            column(b_hi),
            column(b_lo),
            column(b_lo2),
            jnp.zeros((hidden * 8, 29), F32),
        ],
        axis=1,
    ).astype(BF16)
    w2 = pair_w2.T * (LOG2E * 0.5 / GAMMA)
    w2_hi, w2_lo = split(w2)
    wide = lambda w: (w.astype(F32)[:, None, :, None] * eye[None, :, None, :]).reshape(heads * 8, hidden * 8)
    second = jnp.concatenate([wide(w2_hi), wide(w2_lo)], axis=0).astype(BF16)
    return first, second


def shards(
    raw,
    raw_kin,
    reader,
    event_id,
    pre_gain,
    w_query,
    w_key,
    w_value,
    w_out,
    post_gain,
    pair_w1,
    pair_b1,
    pair_w2,
):
    groups = raw.shape[1]
    rows = raw.shape[2]
    width = raw.shape[3]
    blocks = lax.axis_size("blk")
    heads = pair_w2.shape[1]
    place = jnp.stack([lax.axis_index("grp"), lax.axis_index("blk")]).astype(jnp.int32)
    raw = raw[0]
    raw_kin = raw_kin[0]
    message = jax.ShapeDtypeStruct((rows + EXTRA, width), BF16)
    smem = pl.BlockSpec(memory_space=pltpu.SMEM)
    vmem = pl.BlockSpec(memory_space=pltpu.VMEM)
    packed = pl.pallas_call(
        pack_kernel,
        out_shape=[message] * (groups - 1),
        in_specs=[smem, vmem, vmem],
        out_specs=[vmem] * (groups - 1),
        name="pack",
    )(place, raw, raw_kin)
    got = [
        lax.ppermute(packed[s - 1], "grp", [(i, (i + s) % groups) for i in range(groups)])
        for s in range(1, groups)
    ]
    mine = pl.pallas_call(
        select_kernel,
        out_shape=message,
        in_specs=[smem] + [vmem] * (5 + len(got)),
        out_specs=vmem,
        name="choose",
    )(place, raw, raw_kin, reader, event_id, pre_gain[None], *got)
    every = [mine] + [
        lax.ppermute(mine, "blk", [(i, (i + s) % blocks) for i in range(blocks)])
        for s in range(1, blocks)
    ]
    first, second = pair_weights(pair_w1, pair_b1, pair_w2)
    tiles = blocks * rows // TILE
    full = lambda a: pl.BlockSpec(a.shape, lambda i: (0,) * a.ndim)
    operands = [*every, w_query, w_key, w_value, w_out, post_gain[None], first, second]
    encoded = pl.pallas_call(
        lambda *refs: main_kernel(*refs, blocks=blocks, heads=heads),
        out_shape=jax.ShapeDtypeStruct((rows, width), BF16),
        grid=(rows // CHUNK,),
        in_specs=[smem] + [full(a) for a in operands],
        out_specs=pl.BlockSpec((CHUNK, width), lambda i: (i, 0)),
        scratch_shapes=[
            pltpu.VMEM((blocks, width, rows), BF16),
            pltpu.VMEM((blocks, rows, width), BF16),
            pltpu.VMEM((5, blocks, rows), F32),
            pltpu.VMEM((8, blocks, rows), F32),
            pltpu.VMEM((8, CHUNK, LANES), F32),
            pltpu.VMEM((CHUNK // 8, 8 * heads, width), BF16),
            pltpu.VMEM((tiles, CHUNK // 8, 8 * heads, TILE), F32),
            pltpu.VMEM((CHUNK, width), F32),
        ],
        compiler_params=pltpu.CompilerParams(dimension_semantics=("arbitrary",)),
        name="attend",
    )(place, *operands)
    return encoded[None]


def solution(mesh):
    in_specs = (
        P("grp", None, "blk", None),
        P("grp", None, None, "blk"),
        P("grp", "blk"),
        P("grp", "blk"),
        P(),
        P(),
        P(),
        P(),
        P(),
        P(),
        P(),
        P(),
        P(),
    )
    out_specs = P("grp", "blk", None)
    return jax.shard_map(shards, mesh=mesh, in_specs=in_specs, out_specs=out_specs, check_vma=False)
```

```python
import math

import jax
import jax.numpy as jnp
from jax import lax
from jax.experimental import pallas as pl
from jax.experimental.pallas import tpu as pltpu
from jax.sharding import PartitionSpec as P


F32 = jnp.float32
BF16 = jnp.bfloat16
EXTRA = 16
LANES = 128
SPAN = 32
MIB = 1 << 20

SQ = math.sqrt(2.0 / math.pi)
GAMMA = (SQ * 0.044715) ** (1.0 / 3.0)
BETA = SQ / GAMMA
LOG2E = math.log2(math.e)
LN2 = math.log(2.0)


def layer_norm(rows, gain):
    center = rows - jnp.mean(rows, axis=-1, keepdims=True)
    spread = jnp.mean(center * center, axis=-1, keepdims=True)
    return center * lax.rsqrt(spread + 1e-05) * gain


def pack_kernel(raw_ref, kin_ref, *out_refs):
    groups, rows, width = raw_ref.shape
    own = lax.axis_index("grp")
    for step, out in enumerate(out_refs):
        target = lax.rem(own + step, groups)
        out[0:rows, :] = raw_ref[target]
        kin = kin_ref[target]
        out[rows : rows + EXTRA, :] = jnp.concatenate(
            [
                jnp.concatenate([kin, jnp.zeros((4, width - rows), BF16)], axis=1),
                jnp.zeros((EXTRA - 4, width), BF16),
            ],
            axis=0,
        )


def choose_kernel(reader_ref, ids_ref, gain_ref, *refs):
    got = refs[:-1]
    out = refs[-1]
    groups = len(got)
    rows = got[0].shape[0] - EXTRA
    width = got[0].shape[1]
    own = lax.axis_index("grp")
    by_lane = reader_ref[...].astype(F32)
    by_row = jnp.transpose(jnp.broadcast_to(by_lane, (LANES, rows)))
    by_row = jnp.concatenate([by_row] * (width // LANES), axis=1)
    tokens = jnp.zeros((rows, width), F32)
    kin = jnp.zeros((4, rows), F32)
    for step, ref in enumerate(got):
        source = lax.rem(own + groups - step, groups).astype(F32)
        tokens = jnp.where(by_row == source, ref[0:rows, :].astype(F32), tokens)
        kin = jnp.where(by_lane == source, ref[rows : rows + EXTRA, 0:rows].astype(F32)[0:4], kin)
    out[0:rows, :] = layer_norm(tokens, gain_ref[...]).astype(BF16)
    block = jnp.concatenate([kin, ids_ref[...].astype(F32), jnp.zeros((EXTRA - 5, rows), F32)], axis=0)
    block = jnp.concatenate([block, jnp.zeros((EXTRA, width - rows), F32)], axis=1)
    out[rows : rows + EXTRA, :] = block.astype(BF16)


def split(value):
    high = value.astype(BF16)
    return high, (value - high.astype(F32)).astype(BF16)


def weights_kernel(w1_ref, b1_ref, w2_ref, first_ref, second_ref):
    hidden = w1_ref.shape[1]
    heads = w2_ref.shape[1]
    row = lax.broadcasted_iota(jnp.int32, (4, hidden), 0)
    w1 = w1_ref[...] * jnp.where(row == 2, GAMMA, GAMMA * LN2)
    w1_hi, w1_lo = split(w1)
    b1 = b1_ref[...] * GAMMA
    b_hi, b_mid = split(b1)
    b_lo = b1 - b_hi.astype(F32) - b_mid.astype(F32)
    stack = jnp.concatenate(
        [
            w1_hi.astype(F32),
            w1_lo.astype(F32),
            b_hi.astype(F32),
            b_mid.astype(F32),
            b_lo,
            jnp.zeros((5, hidden), F32),
        ],
        axis=0,
    ).astype(BF16)

    def onehot(hit):
        return jnp.where(hit, 1.0, 0.0).astype(BF16)

    def iota(shape, axis):
        return lax.broadcasted_iota(jnp.int32, shape, axis)

    units = hidden * 8
    grown = onehot(iota((hidden, units), 1) // 8 == iota((hidden, units), 0))
    tall = jnp.dot(stack, grown, preferred_element_type=F32).astype(BF16)
    col = iota((16, LANES), 1)
    which = jnp.where(col < 32, col // 8, jnp.where(col < 96, col // 8 - 4, col - 88))
    pick = onehot((which == iota((16, LANES), 0)) & (col < 99))
    first = lax.dot_general(tall, pick, (((0,), (0,)), ((), ())), preferred_element_type=F32)
    col = iota((units, LANES), 1)
    same = (iota((units, LANES), 0) % 8 == col % 8) | (col >= 96)
    first_ref[...] = jnp.where(same, first, 0.0).astype(BF16)

    w2_hi, w2_lo = split(w2_ref[...] * (LOG2E * 0.5 / GAMMA))
    contract = (((0,), (0,)), ((), ()))
    wide = [lax.dot_general(w, grown, contract, preferred_element_type=F32) for w in (w2_hi, w2_lo)]
    wide = jnp.concatenate(wide, axis=0).astype(BF16)
    shape = (16 * heads, 2 * heads)
    lift = onehot(iota(shape, 0) // 8 == iota(shape, 1))
    second = jnp.dot(lift, wide, preferred_element_type=F32)
    shape = (16 * heads, units)
    second_ref[...] = jnp.where(iota(shape, 0) % 8 == iota(shape, 1) % 8, second, 0.0).astype(BF16)


def main_kernel(*refs, flips, heads):
    blocks = len(flips)
    got = refs[:blocks]
    (wq_ref, wk_ref, wv_ref, wo_ref, gain_ref, first_ref, second_ref, out_ref) = refs[blocks : blocks + 8]
    (x_ref, k_ref, v_ref, raw_ref, term_ref, qt_ref, qm_ref, f_ref, act_ref, s_ref, att_ref, lo_ref, hi_ref) = refs[
        blocks + 8 :
    ]
    rows = got[0].shape[0] - EXTRA
    width = got[0].shape[1]
    head_size = width // heads
    total_keys = blocks * rows
    own = lax.axis_index("blk")
    spans = rows // SPAN
    groups = SPAN // 8
    lines = 8 * heads

    for flip, ref in zip(flips, got):
        block = lax.bitwise_xor(own, flip)
        x_ref[block] = ref[0:rows, :]
        extra = ref[rows : rows + EXTRA, 0:rows].astype(F32)
        for row in range(4):
            raw_ref[row, pl.ds(block, 1), :] = extra[row : row + 1, :]
        event = extra[4:5, :]
        if blocks == 8 and flip >= 6:
            inner = jnp.logical_and(own >= 2, own < 6)
            event = jnp.where(inner, event, -1.0)
        raw_ref[4, pl.ds(block, 1), :] = event
    slab = min(8, blocks)

    def project(index, carry):
        at = index * slab
        feats = x_ref[pl.ds(at, slab)].reshape(slab * rows, width)
        k_ref[pl.ds(at, slab)] = (
            jnp.dot(feats, wk_ref[...], preferred_element_type=F32).astype(BF16).reshape(slab, rows, width)
        )
        v_ref[pl.ds(at, slab)] = (
            jnp.dot(feats, wv_ref[...], preferred_element_type=F32).astype(BF16).reshape(slab, rows, width)
        )
        return carry

    lax.fori_loop(0, blocks // slab, project, 0)
    pt = raw_ref[0]
    rap = raw_ref[1]
    phi = raw_ref[2]
    mass = raw_ref[3]
    ids = raw_ref[4]
    m2 = mass * mass
    mt = jnp.sqrt(pt * pt + m2)
    for t, term in enumerate(
        (pt, rap, jnp.cos(phi), jnp.sin(phi), mt * jnp.exp(rap), mt * jnp.exp(-rap), m2, ids)
    ):
        term_ref[t] = term

    mine = jnp.concatenate([term_ref[t, pl.ds(own, 1), :] for t in range(8)], axis=0)
    factor = lax.broadcasted_iota(jnp.int32, (8, rows), 0)
    scaled = jnp.where((factor == 2) | (factor == 3), mine * 2.0, mine)
    scaled = jnp.where(factor == 6, mine + 1.0, scaled)
    cols = jnp.transpose(jnp.concatenate([scaled, jnp.zeros((LANES - 8, rows), F32)], axis=0))
    for t in range(8):
        qt_ref[t] = jnp.broadcast_to(cols[:, t : t + 1], (rows, LANES))
    queries = jnp.dot(got[0][0:rows, :], wq_ref[...], preferred_element_type=F32).astype(BF16).astype(F32)
    lane_head = lax.broadcasted_iota(jnp.int32, (8, width), 1) // head_size
    for g in range(rows // 8):
        piece = queries[8 * g : 8 * g + 8, :]
        qm_ref[g // groups, (g % groups) * lines : (g % groups + 1) * lines, :] = jnp.concatenate(
            [jnp.where(lane_head == h, piece, 0.0) for h in range(heads)], axis=0
        ).astype(BF16)

    least = jnp.min(ids, axis=1, keepdims=True)
    most = jnp.max(ids, axis=1, keepdims=True)
    number = lax.broadcasted_iota(jnp.int32, (blocks, 1), 0).astype(F32)
    lane = lax.broadcasted_iota(jnp.int32, (1, rows), 1) // SPAN
    count = jnp.int32(0)
    for s in range(spans):
        q_ids = mine[7:8, :]
        q_least = jnp.min(jnp.where(lane == s, q_ids, 1e9), axis=1, keepdims=True)
        q_most = jnp.max(jnp.where(lane == s, q_ids, -1e9), axis=1, keepdims=True)
        live = (least <= q_most) & (most >= q_least)
        lo = jnp.min(jnp.where(live, number, 1e9)).astype(jnp.int32)
        hi = jnp.max(jnp.where(live, number, -1.0)).astype(jnp.int32)
        lo_ref[s] = lo
        hi_ref[s] = hi
        count = count + (hi - lo + 1)

        def blank(j, carry, s=s):
            s_ref[j, s] = jnp.full((SPAN * heads, LANES), -1e30, F32)
            return carry

        lax.fori_loop(0, lo, blank, 0)
        lax.fori_loop(hi + 1, blocks, blank, 0)

    f_ref[96:128, :] = jnp.ones((32, groups * LANES), BF16)
    scale = LOG2E * head_size ** (-0.5)

    def features(s, j):
        k = [term_ref[t, pl.ds(j, 1), :] for t in range(7)]
        for g in range(groups):
            at = pl.multiple_of(s * SPAN + 8 * g, 8)
            q = [qt_ref[t, pl.ds(at, 8), :] for t in range(7)]
            gap = q[1] - k[1]
            cos_gap = q[2] * k[2] + q[3] * k[3]
            dist = gap * gap + (2.0 - cos_gap)
            low = jnp.minimum(q[0], k[0])
            pair_mass = (q[6] + k[6]) + (q[4] * k[5] + q[5] * k[4] - (q[0] * k[0]) * cos_gap)
            ab = jnp.concatenate([jnp.log2(1.0 + dist), jnp.log2(1.0 + low * low * dist)], axis=0)
            cd = jnp.concatenate([low / (q[0] + k[0]), jnp.log2(pair_mass)], axis=0)
            ab_hi, ab_lo = split(ab)
            cd_hi, cd_lo = split(cd)
            f_ref[0:96, g * LANES : (g + 1) * LANES] = jnp.concatenate(
                [ab_hi, cd_hi, ab_lo, cd_lo, ab_hi, cd_hi], axis=0
            )

    def activate():
        hidden = jnp.dot(first_ref[...], f_ref[...], preferred_element_type=F32)
        act = hidden * (1.0 + jnp.tanh(hidden * (hidden * hidden + BETA)))
        act_ref[...] = act.astype(BF16)

    def score(s, j):
        bias2 = jnp.dot(second_ref[...], act_ref[...], preferred_element_type=F32)
        bias = bias2[0:lines, :] + bias2[lines:, :]
        match = lax.dot_general(
            qm_ref[s], k_ref[j], (((1,), (1,)), ((), ())), preferred_element_type=F32
        )
        key_ids = term_ref[7, pl.ds(j, 1), :]
        for g in range(groups):
            at = pl.multiple_of(s * SPAN + 8 * g, 8)
            live = qt_ref[7, pl.ds(at, 8), :] == key_ids
            for h in range(heads):
                line = g * lines + 8 * h
                value = match[line : line + 8, :] * scale + bias[8 * h : 8 * h + 8, g * LANES : (g + 1) * LANES]
                s_ref[j, s, line : line + 8, :] = jnp.where(live, value, -1e30)

    def step(index, carry):
        s, j, s1, j1, s2, j2 = carry
        score(s2, j2)
        activate()
        features(s, j)
        ends = j >= hi_ref[s]
        stop = jnp.logical_and(ends, s == spans - 1)
        s_next = jnp.where(stop, s, jnp.where(ends, s + 1, s))
        j_next = jnp.where(stop, j, jnp.where(ends, lo_ref[s_next], j + 1))
        return (s_next, j_next, s, j, s1, j1)

    zero = jnp.int32(0)
    begin = lo_ref[0]
    lax.fori_loop(0, count + 2, step, (zero, begin, zero, begin, zero, begin))

    deep = (SPAN * heads, width)
    diag = (lax.broadcasted_iota(jnp.int32, deep, 0) % lines) // 8 == lax.broadcasted_iota(
        jnp.int32, deep, 1
    ) // head_size

    def attend(s, carry):
        top = s_ref[0, s]
        for j in range(1, blocks):
            top = jnp.maximum(top, s_ref[j, s])
        top = jnp.max(top, axis=1, keepdims=True)
        total = jnp.zeros((SPAN * heads, LANES), F32)
        pieces = []
        for j in range(blocks):
            weights = jnp.exp2(s_ref[j, s] - top)
            total = total + weights
            pieces.append(weights.astype(BF16))
        accum = jnp.dot(
            jnp.concatenate(pieces, axis=1),
            v_ref[...].reshape(total_keys, width),
            preferred_element_type=F32,
        )
        total = jnp.sum(total, axis=1, keepdims=True)
        accum = jnp.where(diag, accum / total, 0.0)
        for g in range(groups):
            out = accum[g * lines : g * lines + 8, :]
            for h in range(1, heads):
                out = out + accum[g * lines + 8 * h : g * lines + 8 * h + 8, :]
            att_ref[pl.ds(pl.multiple_of(s * SPAN + 8 * g, 8), 8), :] = out
        return carry

    lax.fori_loop(0, spans, attend, 0)
    mixed = jnp.dot(att_ref[...].astype(BF16), wo_ref[...], preferred_element_type=F32)
    out_ref[...] = layer_norm(mixed, gain_ref[...]).astype(BF16)


def gather_group(mine, blocks):
    shifts = {8: (4, 2, 6)}.get(blocks, tuple(range(2, blocks, 2)))
    got = [mine]
    flips = [0] + list(shifts)
    for flip in shifts:
        pairs = [(i, i ^ flip) for i in range(blocks)]
        if blocks == 8 and flip == 6:
            pairs = [(i, i ^ flip if 2 <= i < 6 else i) for i in range(blocks)]
        got.append(lax.ppermute(mine, "blk", pairs))
    near = [(i, i ^ 1) for i in range(blocks)]
    got += [lax.ppermute(part, "blk", near) for part in list(got)]
    flips += [flip ^ 1 for flip in flips]
    return got, flips


def shards(
    raw,
    raw_kin,
    reader,
    event_id,
    pre_gain,
    w_query,
    w_key,
    w_value,
    w_out,
    post_gain,
    pair_w1,
    pair_b1,
    pair_w2,
):
    groups = raw.shape[1]
    rows = raw.shape[2]
    width = raw.shape[3]
    blocks = lax.axis_size("blk")
    heads = pair_w2.shape[1]
    assert rows == LANES and blocks & (blocks - 1) == 0
    raw = raw[0]
    raw_kin = raw_kin[0]
    message = jax.ShapeDtypeStruct((rows + EXTRA, width), BF16)
    vmem = pl.BlockSpec(memory_space=pltpu.VMEM)
    small = pltpu.CompilerParams(vmem_limit_bytes=8 * MIB)
    packed = pl.pallas_call(
        pack_kernel,
        out_shape=[message] * groups,
        in_specs=[vmem, vmem],
        out_specs=[vmem] * groups,
        compiler_params=small,
        name="pack",
    )(raw, raw_kin)
    parts = [packed[0]] + [
        lax.ppermute(packed[s], "grp", [(i, (i + s) % groups) for i in range(groups)])
        for s in range(1, groups)
    ]
    mine = pl.pallas_call(
        choose_kernel,
        out_shape=message,
        in_specs=[vmem] * (3 + groups),
        out_specs=vmem,
        compiler_params=small,
        name="choose",
    )(reader, event_id, pre_gain[None], *parts)
    got, flips = gather_group(mine, blocks)
    hidden = pair_w1.shape[1]
    first, second = pl.pallas_call(
        weights_kernel,
        out_shape=[
            jax.ShapeDtypeStruct((8 * hidden, LANES), BF16),
            jax.ShapeDtypeStruct((16 * heads, 8 * hidden), BF16),
        ],
        in_specs=[vmem] * 3,
        out_specs=[vmem] * 2,
        compiler_params=small,
        name="weights",
    )(pair_w1, pair_b1[None], pair_w2)
    operands = [*got, w_query, w_key, w_value, w_out, post_gain[None], first, second]
    spans = rows // SPAN
    lanes = SPAN // 8 * LANES
    encoded = pl.pallas_call(
        lambda *refs: main_kernel(*refs, flips=flips, heads=heads),
        out_shape=jax.ShapeDtypeStruct((rows, width), BF16),
        in_specs=[vmem] * len(operands),
        out_specs=vmem,
        scratch_shapes=[
            pltpu.VMEM((blocks, rows, width), BF16),
            pltpu.VMEM((blocks, rows, width), BF16),
            pltpu.VMEM((blocks, rows, width), BF16),
            pltpu.VMEM((5, blocks, rows), F32),
            pltpu.VMEM((8, blocks, rows), F32),
            pltpu.VMEM((8, rows, LANES), F32),
            pltpu.VMEM((spans, SPAN * heads, width), BF16),
            pltpu.VMEM((LANES, lanes), BF16),
            pltpu.VMEM((8 * hidden, lanes), BF16),
            pltpu.VMEM((blocks, spans, SPAN * heads, LANES), F32),
            pltpu.VMEM((rows, width), F32),
            pltpu.SMEM((spans,), jnp.int32),
            pltpu.SMEM((spans,), jnp.int32),
        ],
        compiler_params=pltpu.CompilerParams(vmem_limit_bytes=(12 + 3 * blocks // 2) * MIB),
        name="attend",
    )(*operands)
    return encoded[None]


def solution(mesh):
    in_specs = (
        P("grp", None, "blk", None),
        P("grp", None, None, "blk"),
        P("grp", "blk"),
        P("grp", "blk"),
        P(),
        P(),
        P(),
        P(),
        P(),
        P(),
        P(),
        P(),
        P(),
    )
    out_specs = P("grp", "blk", None)
    return jax.shard_map(shards, mesh=mesh, in_specs=in_specs, out_specs=out_specs, check_vma=False)
```

```python
import math

import jax
import jax.numpy as jnp
from jax import lax
from jax.experimental import pallas as pl
from jax.experimental.pallas import tpu as pltpu
from jax.sharding import PartitionSpec as P


F32 = jnp.float32
BF16 = jnp.bfloat16
EXTRA = 16
LANES = 128
SPAN = 32
MIB = 1 << 20

SQ = math.sqrt(2.0 / math.pi)
GAMMA = (SQ * 0.044715) ** (1.0 / 3.0)
BETA = SQ / GAMMA
LOG2E = math.log2(math.e)
LN2 = math.log(2.0)


def iota(shape, axis):
    return lax.broadcasted_iota(jnp.int32, shape, axis)


def layer_norm(rows, gain):
    center = rows - jnp.mean(rows, axis=-1, keepdims=True)
    spread = jnp.mean(center * center, axis=-1, keepdims=True)
    return center * lax.rsqrt(spread + 1e-05) * gain


def pack_kernel(raw_ref, kin_ref, reader_ref, ids_ref, pre_ref, post_ref, *refs):
    groups, rows, width = raw_ref.shape
    messages = refs[:groups]
    copies = refs[groups : groups + 4]
    kin_own, sems = refs[groups + 4 :]
    own = lax.axis_index("grp")
    moves = [
        pltpu.make_async_copy(raw_ref.at[lax.rem(own + step, groups)], out.at[pl.ds(0, rows)], sems.at[step])
        for step, out in enumerate(messages)
    ]
    first = pltpu.make_async_copy(kin_ref, kin_own, sems.at[groups])
    first.start()
    for move in moves:
        move.start()
    others = [
        pltpu.make_async_copy(source, out, sems.at[groups + 1 + at])
        for at, (source, out) in enumerate(zip((reader_ref, ids_ref, pre_ref, post_ref), copies))
    ]
    for move in others:
        move.start()
    first.wait()
    for step, out in enumerate(messages):
        kin = kin_own[lax.rem(own + step, groups)]
        out[rows : rows + EXTRA, :] = jnp.concatenate(
            [
                jnp.concatenate([kin, jnp.zeros((4, width - rows), BF16)], axis=1),
                jnp.zeros((EXTRA - 4, width), BF16),
            ],
            axis=0,
        )
    for move in moves + others:
        move.wait()


def choose_kernel(reader_ref, ids_ref, gain_ref, ready_ref, *refs):
    got = refs[:-1]
    out = refs[-1]
    groups = len(got)
    rows = got[0].shape[0] - EXTRA
    width = got[0].shape[1]
    own = lax.axis_index("grp")
    by_lane = reader_ref[...].astype(F32)
    by_row = jnp.transpose(jnp.broadcast_to(by_lane, (LANES, rows)))
    by_row = jnp.concatenate([by_row] * (width // LANES), axis=1)
    tokens = jnp.zeros((rows, width), F32)
    kin = jnp.zeros((4, rows), F32)
    for step, ref in enumerate(got):
        source = lax.rem(own + groups - step, groups).astype(F32)
        tokens = jnp.where(by_row == source, ref[0:rows, :].astype(F32), tokens)
        kin = jnp.where(by_lane == source, ref[rows : rows + EXTRA, 0:rows].astype(F32)[0:4], kin)
    out[0:rows, :] = layer_norm(tokens, gain_ref[...]).astype(BF16)
    block = jnp.concatenate([kin, ids_ref[...].astype(F32), jnp.zeros((EXTRA - 5, rows), F32)], axis=0)
    block = jnp.concatenate([block, jnp.zeros((EXTRA, width - rows), F32)], axis=1)
    out[rows : rows + EXTRA, :] = block.astype(BF16)


def split(value):
    high = value.astype(BF16)
    return high, (value - high.astype(F32)).astype(BF16)


def weights_kernel(*refs):
    sources = refs[:7]
    copies = refs[7:11]
    first_ref, second_ref, w1_ref, b1_ref, w2_ref, sems = refs[11:]
    moves = [
        pltpu.make_async_copy(source, out, sems.at[at])
        for at, (source, out) in enumerate(zip(sources, (w1_ref, b1_ref, w2_ref, *copies)))
    ]
    for move in moves:
        move.start()
    for move in moves[:3]:
        move.wait()
    hidden = w1_ref.shape[1]
    heads = w2_ref.shape[0]
    row = lax.broadcasted_iota(jnp.int32, (4, hidden), 0)
    w1 = w1_ref[...] * jnp.where(row == 2, GAMMA, GAMMA * LN2)
    w1_hi, w1_lo = split(w1)
    b1 = b1_ref[...] * GAMMA
    b_hi, b_mid = split(b1)
    b_lo = b1 - b_hi.astype(F32) - b_mid.astype(F32)
    stack = jnp.concatenate(
        [
            w1_hi.astype(F32),
            w1_lo.astype(F32),
            b_hi.astype(F32),
            b_mid.astype(F32),
            b_lo,
            jnp.zeros((5, hidden), F32),
        ],
        axis=0,
    ).astype(BF16)

    def onehot(hit):
        return jnp.where(hit, 1.0, 0.0).astype(BF16)

    units = hidden * 8
    grown = onehot(iota((hidden, units), 1) // 8 == iota((hidden, units), 0))
    tall = jnp.dot(stack, grown, preferred_element_type=F32).astype(BF16)
    col = iota((16, LANES), 1)
    which = jnp.where(col < 32, col // 8, jnp.where(col < 96, col // 8 - 4, col - 88))
    pick = onehot((which == iota((16, LANES), 0)) & (col < 99))
    first = lax.dot_general(tall, pick, (((0,), (0,)), ((), ())), preferred_element_type=F32)
    col = iota((units, LANES), 1)
    same = (iota((units, LANES), 0) % 8 == col % 8) | (col >= 96)
    first_ref[...] = jnp.where(same, first, 0.0).astype(BF16)

    w2_hi, w2_lo = split(w2_ref[...] * (LOG2E * 0.5 / GAMMA))
    wide = [jnp.dot(w, grown, preferred_element_type=F32) for w in (w2_hi, w2_lo)]
    wide = jnp.concatenate(wide, axis=0).astype(BF16)
    shape = (16 * heads, 2 * heads)
    lift = onehot(iota(shape, 0) // 8 == iota(shape, 1))
    second = jnp.dot(lift, wide, preferred_element_type=F32)
    shape = (16 * heads, units)
    second_ref[...] = jnp.where(iota(shape, 0) % 8 == iota(shape, 1) % 8, second, 0.0).astype(BF16)
    for move in moves[3:]:
        move.wait()


def key_side(got, checks, wk_ref, wv_ref, x_ref, k_ref, v_ref, raw_ref, term_ref):
    count = len(got)
    rows = got[0].shape[0] - EXTRA
    width = got[0].shape[1]
    for place, (ref, check) in enumerate(zip(got, checks)):
        x_ref[place] = ref[0:rows, :]
        extra = ref[rows : rows + EXTRA, 0:rows].astype(F32)
        for row in range(4):
            raw_ref[row, place : place + 1, :] = extra[row : row + 1, :]
        event = extra[4:5, :]
        raw_ref[4, place : place + 1, :] = event if check is None else jnp.where(check, event, -1.0)
    feats = x_ref[...].reshape(count * rows, width)
    shape = (count, rows, width)
    k_ref[...] = jnp.dot(feats, wk_ref[...], preferred_element_type=F32).astype(BF16).reshape(shape)
    v_ref[...] = jnp.dot(feats, wv_ref[...], preferred_element_type=F32).astype(BF16).reshape(shape)
    pt = raw_ref[0]
    rap = raw_ref[1]
    phi = raw_ref[2]
    mass = raw_ref[3]
    m2 = mass * mass
    mt = jnp.sqrt(pt * pt + m2)
    terms = (pt, rap, jnp.cos(phi), jnp.sin(phi), mt * jnp.exp(rap), mt * jnp.exp(-rap), m2, raw_ref[4])
    for t, term in enumerate(terms):
        term_ref[t] = term


def query_side(mine_ref, wq_ref, term_ref, qt_ref, qm_ref, heads):
    rows = mine_ref.shape[0] - EXTRA
    width = mine_ref.shape[1]
    groups = SPAN // 8
    lines = 8 * heads
    mine = jnp.concatenate([term_ref[t, 0:1, :] for t in range(8)], axis=0)
    factor = iota((8, rows), 0)
    scaled = jnp.where((factor == 2) | (factor == 3), mine * 2.0, mine)
    scaled = jnp.where(factor == 6, mine + 1.0, scaled)
    cols = jnp.transpose(jnp.concatenate([scaled, jnp.zeros((LANES - 8, rows), F32)], axis=0))
    for t in range(8):
        qt_ref[t] = jnp.broadcast_to(cols[:, t : t + 1], (rows, LANES))
    queries = jnp.dot(mine_ref[0:rows, :], wq_ref[...], preferred_element_type=F32).astype(BF16).astype(F32)
    lane_head = iota((8, width), 1) // (width // heads)
    for g in range(rows // 8):
        piece = queries[8 * g : 8 * g + 8, :]
        qm_ref[g // groups, (g % groups) * lines : (g % groups + 1) * lines, :] = jnp.concatenate(
            [jnp.where(lane_head == h, piece, 0.0) for h in range(heads)], axis=0
        ).astype(BF16)


def pair_scores(
    mine_ref, first_ref, second_ref, qt_ref, qm_ref, k_ref, term_ref, f_ref, h_ref, act_ref, s_ref, table_ref, heads
):
    blocks, rows, width = k_ref.shape
    spans = rows // SPAN
    groups = SPAN // 8
    lines = 8 * heads
    scale = LOG2E * (width // heads) ** (-0.5)

    ids = term_ref[7]
    least = jnp.min(ids, axis=1, keepdims=True)
    most = jnp.max(ids, axis=1, keepdims=True)
    weight = jnp.left_shift(1, iota((blocks, 1), 0)).astype(F32)
    q_ids = mine_ref[rows : rows + EXTRA, 0:rows].astype(F32)[4:5, :]
    lane = iota((1, rows), 1) // SPAN
    count = jnp.int32(0)
    for s in range(spans):
        q_least = jnp.min(jnp.where(lane == s, q_ids, 1e9), axis=1, keepdims=True)
        q_most = jnp.max(jnp.where(lane == s, q_ids, -1e9), axis=1, keepdims=True)
        live = (least <= q_most) & (most >= q_least)
        bits = jnp.sum(jnp.where(live, weight, 0.0)).astype(jnp.int32)
        for place in range(blocks):
            bit = lax.bitwise_and(lax.shift_right_logical(bits, place), 1)
            table_ref[count] = jnp.int32(16 * s + place)
            count = count + bit

            @pl.when(bit == 0)
            def blank(place=place, s=s):
                s_ref[place, s] = jnp.full((SPAN * heads, LANES), -1e30, F32)

    f_ref[:, 96:128, :] = jnp.ones((2, 32, groups * LANES), BF16)

    def features(side, s, j):
        k = [term_ref[t, pl.ds(j, 1), :] for t in range(7)]
        for g in range(groups):
            at = pl.multiple_of(s * SPAN + 8 * g, 8)
            q = [qt_ref[t, pl.ds(at, 8), :] for t in range(7)]
            gap = q[1] - k[1]
            cos_gap = q[2] * k[2] + q[3] * k[3]
            dist = gap * gap + (2.0 - cos_gap)
            low = jnp.minimum(q[0], k[0])
            pair_mass = (q[6] + k[6]) + (q[4] * k[5] + q[5] * k[4] - (q[0] * k[0]) * cos_gap)
            ab = jnp.concatenate([jnp.log2(1.0 + dist), jnp.log2(1.0 + low * low * dist)], axis=0)
            cd = jnp.concatenate([low / (q[0] + k[0]), jnp.log2(pair_mass)], axis=0)
            ab_hi, ab_lo = split(ab)
            cd_hi, cd_lo = split(cd)
            f_ref[side, 0:96, g * LANES : (g + 1) * LANES] = jnp.concatenate(
                [ab_hi, cd_hi, ab_lo, cd_lo, ab_hi, cd_hi], axis=0
            )

    def activate(side):
        hidden = h_ref[side]
        act = hidden * (1.0 + jnp.tanh(hidden * (hidden * hidden + BETA)))
        act_ref[side] = act.astype(BF16)

    def score(side, s, j):
        bias2 = jnp.dot(second_ref[...], act_ref[side], preferred_element_type=F32)
        bias = bias2[0:lines, :] + bias2[lines:, :]
        match = lax.dot_general(
            qm_ref[s], k_ref[j], (((1,), (1,)), ((), ())), preferred_element_type=F32
        )
        key_ids = term_ref[7, pl.ds(j, 1), :]
        for g in range(groups):
            at = pl.multiple_of(s * SPAN + 8 * g, 8)
            live = qt_ref[7, pl.ds(at, 8), :] == key_ids
            for h in range(heads):
                line = g * lines + 8 * h
                value = match[line : line + 8, :] * scale + bias[8 * h : 8 * h + 8, g * LANES : (g + 1) * LANES]
                s_ref[j, s, line : line + 8, :] = jnp.where(live, value, -1e30)

    def task(at):
        code = table_ref[jnp.clip(at, 0, count - 1)]
        return lax.shift_right_logical(code, 4), lax.bitwise_and(code, 15)

    def step(index, carry):
        for side in range(2):
            at = 2 * index + side
            score(1 - side, *task(at - 3))
            activate(side)
            h_ref[1 - side] = jnp.dot(first_ref[...], f_ref[1 - side], preferred_element_type=F32)
            features(side, *task(at))
        return carry

    lax.fori_loop(0, jnp.where(count > 0, (count + 4) // 2, 0), step, 0)


def own_kernel(mine_ref, wq_ref, wk_ref, wv_ref, first_ref, second_ref, s_ref, v_ref, qt_ref, qm_ref, *scratch, heads):
    x_ref, k_ref, raw_ref, term_ref, f_ref, h_ref, act_ref, table_ref = scratch
    key_side([mine_ref], [None], wk_ref, wv_ref, x_ref, k_ref, v_ref, raw_ref, term_ref)
    query_side(mine_ref, wq_ref, term_ref, qt_ref, qm_ref, heads)
    pair_scores(
        mine_ref, first_ref, second_ref, qt_ref, qm_ref, k_ref, term_ref, f_ref, h_ref, act_ref, s_ref, table_ref, heads
    )


def inner_block(blocks):
    own = lax.axis_index("blk")
    return jnp.logical_and(own >= 2, own < blocks - 2)


def near_kernel(mine_ref, *refs, flips, blocks, heads):
    count = len(flips)
    got = refs[:count]
    wk_ref, wv_ref, first_ref, second_ref, qt_ref, qm_ref, s_ref, v_ref = refs[count : count + 8]
    x_ref, k_ref, raw_ref, term_ref, f_ref, h_ref, act_ref, table_ref = refs[count + 8 :]
    checks = [inner_block(blocks) if blocks == 8 and flip >= 6 else None for flip in flips]
    key_side(got, checks, wk_ref, wv_ref, x_ref, k_ref, v_ref, raw_ref, term_ref)
    pair_scores(
        mine_ref, first_ref, second_ref, qt_ref, qm_ref, k_ref, term_ref, f_ref, h_ref, act_ref, s_ref, table_ref, heads
    )


def last_kernel(mine_ref, *refs, flips, blocks, heads):
    count = len(flips)
    got = refs[:count]
    wk_ref, wv_ref, first_ref, second_ref, qt_ref, qm_ref = refs[count : count + 6]
    s_own, s_near, v_own, v_near, wo_ref, gain_ref, out_ref = refs[count + 6 : count + 13]
    x_ref, k_ref, raw_ref, term_ref, f_ref, h_ref, act_ref, table_ref, s_ref, v_ref, att_ref = refs[count + 13 :]
    checks = [inner_block(blocks) if blocks == 8 and flip >= 6 else None for flip in flips]
    key_side(got, checks, wk_ref, wv_ref, x_ref, k_ref, v_ref, raw_ref, term_ref)
    pair_scores(
        mine_ref, first_ref, second_ref, qt_ref, qm_ref, k_ref, term_ref, f_ref, h_ref, act_ref, s_ref, table_ref, heads
    )
    rows = out_ref.shape[0]
    width = out_ref.shape[1]
    lines = 8 * heads
    deep = (SPAN * heads, width)
    diag = (iota(deep, 0) % lines) // 8 == iota(deep, 1) // (width // heads)
    parts = [(s_own, v_own), (s_near, v_near), (s_ref, v_ref)]

    def attend(s, carry):
        top = None
        for scores, _ in parts:
            for j in range(scores.shape[0]):
                top = scores[j, s] if top is None else jnp.maximum(top, scores[j, s])
        top = jnp.max(top, axis=1, keepdims=True)
        total = jnp.zeros((SPAN * heads, LANES), F32)
        accum = jnp.zeros(deep, F32)
        for scores, values in parts:
            pieces = []
            for j in range(scores.shape[0]):
                weights = jnp.exp2(scores[j, s] - top)
                total = total + weights
                pieces.append(weights.astype(BF16))
            accum = accum + jnp.dot(
                jnp.concatenate(pieces, axis=1),
                values[...].reshape(len(pieces) * rows, width),
                preferred_element_type=F32,
            )
        total = jnp.sum(total, axis=1, keepdims=True)
        accum = jnp.where(diag, accum / total, 0.0)
        for g in range(SPAN // 8):
            out = accum[g * lines : g * lines + 8, :]
            for h in range(1, heads):
                out = out + accum[g * lines + 8 * h : g * lines + 8 * h + 8, :]
            att_ref[pl.ds(pl.multiple_of(s * SPAN + 8 * g, 8), 8), :] = out
        return carry

    lax.fori_loop(0, rows // SPAN, attend, 0)
    mixed = jnp.dot(att_ref[...].astype(BF16), wo_ref[...], preferred_element_type=F32)
    out_ref[...] = layer_norm(mixed, gain_ref[...]).astype(BF16)


def shards(
    raw,
    raw_kin,
    reader,
    event_id,
    pre_gain,
    w_query,
    w_key,
    w_value,
    w_out,
    post_gain,
    pair_w1,
    pair_b1,
    pair_w2,
):
    groups = raw.shape[1]
    rows = raw.shape[2]
    width = raw.shape[3]
    blocks = lax.axis_size("blk")
    heads = pair_w2.shape[1]
    hidden = pair_w1.shape[1]
    assert rows == LANES and blocks & (blocks - 1) == 0 and blocks <= 32
    raw = raw[0]
    raw_kin = raw_kin[0]
    array = jax.ShapeDtypeStruct
    message = array((rows + EXTRA, width), BF16)
    vmem = pl.BlockSpec(memory_space=pltpu.VMEM)
    hbm = pl.BlockSpec(memory_space=pltpu.HBM)

    def call(kernel, name, out_shape, operands, scratch=(), limit=8, specs=None):
        single = not isinstance(out_shape, list)
        return pl.pallas_call(
            kernel,
            out_shape=out_shape,
            in_specs=specs or [vmem] * len(operands),
            out_specs=vmem if single else [vmem] * len(out_shape),
            scratch_shapes=list(scratch),
            compiler_params=pltpu.CompilerParams(vmem_limit_bytes=limit * MIB),
            name=name,
        )(*[pltpu.with_memory_space_constraint(a, pltpu.HBM) for a in operands] if specs else operands)

    small = [reader, event_id, pre_gain[None], post_gain[None]]
    packed = call(
        pack_kernel,
        "pack",
        [message] * groups + [array(a.shape, a.dtype) for a in small],
        [raw, raw_kin, *small],
        [pltpu.VMEM(raw_kin.shape, BF16), pltpu.SemaphoreType.DMA((groups + 5,))],
        specs=[hbm] * 6,
    )
    reader, event_id, pre_row, post_row = packed[groups:]
    parts = [packed[0]] + [
        lax.ppermute(packed[s], "grp", [(i, (i + s) % groups) for i in range(groups)])
        for s in range(1, groups)
    ]
    local = [pair_w1, pair_b1[None], pair_w2.T]
    dense = [w_query, w_key, w_value, w_out]
    w_query, w_key, w_value, w_out, first, second = call(
        weights_kernel,
        "weights",
        [array(a.shape, a.dtype) for a in dense]
        + [array((8 * hidden, LANES), BF16), array((16 * heads, 8 * hidden), BF16)],
        local + dense,
        [pltpu.VMEM(a.shape, a.dtype) for a in local] + [pltpu.SemaphoreType.DMA((7,))],
        specs=[hbm] * 7,
    )
    mine = call(choose_kernel, "choose", message, [reader, event_id, pre_row, first, *parts])

    shifts = list({8: (4, 2, 6)}.get(blocks, range(2, blocks, 2)))
    aside = [(i, i ^ 1) for i in range(blocks)]
    along = []
    for flip in shifts:
        pairs = [(i, i ^ flip) for i in range(blocks)]
        if blocks == 8 and flip == 6:
            pairs = [(i, i ^ flip if 2 <= i < 6 else i) for i in range(blocks)]
        along.append(lax.ppermute(mine, "blk", pairs))
    beside = lax.ppermute(mine, "blk", aside)

    spans = rows // SPAN
    lanes = SPAN // 8 * LANES
    tall = SPAN * heads

    def scratch(count):
        return [
            pltpu.VMEM((count, rows, width), BF16),
            pltpu.VMEM((count, rows, width), BF16),
            pltpu.VMEM((5, count, rows), F32),
            pltpu.VMEM((8, count, rows), F32),
            pltpu.VMEM((2, LANES, lanes), BF16),
            pltpu.VMEM((2, 8 * hidden, lanes), F32),
            pltpu.VMEM((2, 8 * hidden, lanes), BF16),
            pltpu.SMEM((spans * count + 1,), jnp.int32),
        ]

    def results(count):
        return [array((count, spans, tall, LANES), F32), array((count, rows, width), BF16)]

    s_own, v_own, q_terms, q_heads = call(
        lambda *refs: own_kernel(*refs, heads=heads),
        "own",
        results(1) + [array((8, rows, LANES), F32), array((spans, tall, width), BF16)],
        [mine, w_query, w_key, w_value, first, second],
        scratch(1),
        limit=10,
    )
    held = lax.optimization_barrier((q_terms, *along))
    q_terms, along = held[0], list(held[1:])
    far = [lax.ppermute(part, "blk", aside) for part in along]
    flips = [1] + shifts
    s_near, v_near = call(
        lambda *refs: near_kernel(*refs, flips=flips, blocks=blocks, heads=heads),
        "near",
        results(len(flips)),
        [mine, beside, *along, w_key, w_value, first, second, q_terms, q_heads],
        scratch(len(flips)),
        limit=12 + blocks // 2,
    )
    flips = [flip ^ 1 for flip in shifts]
    far_scratch = scratch(len(flips))
    far_shapes = [
        pltpu.VMEM((len(flips), spans, tall, LANES), F32),
        pltpu.VMEM((len(flips), rows, width), BF16),
        pltpu.VMEM((rows, width), F32),
    ]
    encoded = call(
        lambda *refs: last_kernel(*refs, flips=flips, blocks=blocks, heads=heads),
        "last",
        array((rows, width), BF16),
        [mine, *far, w_key, w_value, first, second, q_terms, q_heads]
        + [s_own, s_near, v_own, v_near, w_out, post_row],
        far_scratch + far_shapes,
        limit=14 + 3 * blocks // 2,
    )
    return encoded[None]


def solution(mesh):
    in_specs = (
        P("grp", None, "blk", None),
        P("grp", None, None, "blk"),
        P("grp", "blk"),
        P("grp", "blk"),
        P(),
        P(),
        P(),
        P(),
        P(),
        P(),
        P(),
        P(),
        P(),
    )
    out_specs = P("grp", "blk", None)
    return jax.shard_map(shards, mesh=mesh, in_specs=in_specs, out_specs=out_specs, check_vma=False)
```

```python
import math

import jax
import jax.numpy as jnp
from jax import lax
from jax.experimental import pallas as pl
from jax.experimental.pallas import tpu as pltpu
from jax.sharding import PartitionSpec as P


F32 = jnp.float32
BF16 = jnp.bfloat16
EXTRA = 16
LANES = 128
SPAN = 32
MIB = 1 << 20

SQ = math.sqrt(2.0 / math.pi)
GAMMA = (SQ * 0.044715) ** (1.0 / 3.0)
BETA = SQ / GAMMA
LOG2E = math.log2(math.e)
LN2 = math.log(2.0)


def iota(shape, axis):
    return lax.broadcasted_iota(jnp.int32, shape, axis)


def layer_norm(rows, gain):
    center = rows - jnp.mean(rows, axis=-1, keepdims=True)
    spread = jnp.mean(center * center, axis=-1, keepdims=True)
    return center * lax.rsqrt(spread + 1e-05) * gain


def pack_kernel(raw_ref, kin_ref, reader_ref, ids_ref, pre_ref, post_ref, *refs):
    groups, rows, width = raw_ref.shape
    messages = refs[:groups]
    copies = refs[groups : groups + 4]
    kin_own, sems = refs[groups + 4 :]
    own = lax.axis_index("grp")
    moves = [
        pltpu.make_async_copy(raw_ref.at[lax.rem(own + step, groups)], out.at[pl.ds(0, rows)], sems.at[step])
        for step, out in enumerate(messages)
    ]
    first = pltpu.make_async_copy(kin_ref, kin_own, sems.at[groups])
    first.start()
    for move in moves:
        move.start()
    others = [
        pltpu.make_async_copy(source, out, sems.at[groups + 1 + at])
        for at, (source, out) in enumerate(zip((reader_ref, ids_ref, pre_ref, post_ref), copies))
    ]
    for move in others:
        move.start()
    first.wait()
    for step, out in enumerate(messages):
        kin = kin_own[lax.rem(own + step, groups)]
        out[rows : rows + EXTRA, :] = jnp.concatenate(
            [
                jnp.concatenate([kin, jnp.zeros((4, width - rows), BF16)], axis=1),
                jnp.zeros((EXTRA - 4, width), BF16),
            ],
            axis=0,
        )
    for move in moves + others:
        move.wait()


def choose_kernel(reader_ref, ids_ref, gain_ref, ready_ref, *refs):
    got = refs[:-1]
    out = refs[-1]
    groups = len(got)
    rows = got[0].shape[0] - EXTRA
    width = got[0].shape[1]
    own = lax.axis_index("grp")
    by_lane = reader_ref[...].astype(F32)
    by_row = jnp.transpose(jnp.broadcast_to(by_lane, (LANES, rows)))
    by_row = jnp.concatenate([by_row] * (width // LANES), axis=1)
    tokens = jnp.zeros((rows, width), F32)
    kin = jnp.zeros((4, rows), F32)
    for step, ref in enumerate(got):
        source = lax.rem(own + groups - step, groups).astype(F32)
        tokens = jnp.where(by_row == source, ref[0:rows, :].astype(F32), tokens)
        kin = jnp.where(by_lane == source, ref[rows : rows + EXTRA, 0:rows].astype(F32)[0:4], kin)
    out[0:rows, :] = layer_norm(tokens, gain_ref[...]).astype(BF16)
    block = jnp.concatenate([kin, ids_ref[...].astype(F32), jnp.zeros((EXTRA - 5, rows), F32)], axis=0)
    block = jnp.concatenate([block, jnp.zeros((EXTRA, width - rows), F32)], axis=1)
    out[rows : rows + EXTRA, :] = block.astype(BF16)


def split(value):
    high = value.astype(BF16)
    return high, (value - high.astype(F32)).astype(BF16)


def weights_kernel(*refs):
    sources = refs[:7]
    copies = refs[7:11]
    first_ref, second_ref, w1_ref, b1_ref, w2_ref, sems = refs[11:]
    moves = [
        pltpu.make_async_copy(source, out, sems.at[at])
        for at, (source, out) in enumerate(zip(sources, (w1_ref, b1_ref, w2_ref, *copies)))
    ]
    for move in moves:
        move.start()
    for move in moves[:3]:
        move.wait()
    hidden = w1_ref.shape[1]
    heads = w2_ref.shape[0]
    row = lax.broadcasted_iota(jnp.int32, (4, hidden), 0)
    w1 = w1_ref[...] * jnp.where(row == 2, GAMMA, GAMMA * LN2)
    w1_hi, w1_lo = split(w1)
    b1 = b1_ref[...] * GAMMA
    b_hi, b_mid = split(b1)
    b_lo = b1 - b_hi.astype(F32) - b_mid.astype(F32)
    stack = jnp.concatenate(
        [
            w1_hi.astype(F32),
            w1_lo.astype(F32),
            b_hi.astype(F32),
            b_mid.astype(F32),
            b_lo,
            jnp.zeros((5, hidden), F32),
        ],
        axis=0,
    ).astype(BF16)

    def onehot(hit):
        return jnp.where(hit, 1.0, 0.0).astype(BF16)

    units = hidden * 8
    grown = onehot(iota((hidden, units), 1) // 8 == iota((hidden, units), 0))
    tall = jnp.dot(stack, grown, preferred_element_type=F32).astype(BF16)
    col = iota((16, LANES), 1)
    which = jnp.where(col < 32, col // 8, jnp.where(col < 96, col // 8 - 4, col - 88))
    pick = onehot((which == iota((16, LANES), 0)) & (col < 99))
    first = lax.dot_general(tall, pick, (((0,), (0,)), ((), ())), preferred_element_type=F32)
    col = iota((units, LANES), 1)
    same = (iota((units, LANES), 0) % 8 == col % 8) | (col >= 96)
    first_ref[...] = jnp.where(same, first, 0.0).astype(BF16)

    w2_hi, w2_lo = split(w2_ref[...] * (LOG2E * 0.5 / GAMMA))
    wide = [jnp.dot(w, grown, preferred_element_type=F32) for w in (w2_hi, w2_lo)]
    wide = jnp.concatenate(wide, axis=0).astype(BF16)
    shape = (16 * heads, 2 * heads)
    lift = onehot(iota(shape, 0) // 8 == iota(shape, 1))
    second = jnp.dot(lift, wide, preferred_element_type=F32)
    shape = (16 * heads, units)
    second_ref[...] = jnp.where(iota(shape, 0) % 8 == iota(shape, 1) % 8, second, 0.0).astype(BF16)
    for move in moves[3:]:
        move.wait()


def key_side(got, checks, wk_ref, wv_ref, x_ref, k_ref, v_ref, raw_ref, term_ref):
    count = len(got)
    rows = got[0].shape[0] - EXTRA
    width = got[0].shape[1]
    for place, (ref, check) in enumerate(zip(got, checks)):
        x_ref[place] = ref[0:rows, :]
        extra = ref[rows : rows + EXTRA, 0:rows].astype(F32)
        for row in range(4):
            raw_ref[row, place : place + 1, :] = extra[row : row + 1, :]
        event = extra[4:5, :]
        raw_ref[4, place : place + 1, :] = event if check is None else jnp.where(check, event, -1.0)
    feats = x_ref[...].reshape(count * rows, width)
    shape = (count, rows, width)
    k_ref[...] = jnp.dot(feats, wk_ref[...], preferred_element_type=F32).astype(BF16).reshape(shape)
    v_ref[...] = jnp.dot(feats, wv_ref[...], preferred_element_type=F32).astype(BF16).reshape(shape)
    pt = raw_ref[0]
    rap = raw_ref[1]
    phi = raw_ref[2]
    mass = raw_ref[3]
    m2 = mass * mass
    mt = jnp.sqrt(pt * pt + m2)
    terms = (pt, rap, jnp.cos(phi), jnp.sin(phi), mt * jnp.exp(rap), mt * jnp.exp(-rap), m2, raw_ref[4])
    for t, term in enumerate(terms):
        term_ref[t] = term


def query_side(mine_ref, wq_ref, term_ref, qt_ref, qm_ref, heads):
    rows = mine_ref.shape[0] - EXTRA
    width = mine_ref.shape[1]
    groups = SPAN // 8
    lines = 8 * heads
    mine = jnp.concatenate([term_ref[t, 0:1, :] for t in range(8)], axis=0)
    factor = iota((8, rows), 0)
    scaled = jnp.where((factor == 2) | (factor == 3), mine * 2.0, mine)
    scaled = jnp.where(factor == 6, mine + 1.0, scaled)
    cols = jnp.transpose(jnp.concatenate([scaled, jnp.zeros((LANES - 8, rows), F32)], axis=0))
    for t in range(8):
        qt_ref[t] = jnp.broadcast_to(cols[:, t : t + 1], (rows, LANES))
    queries = jnp.dot(mine_ref[0:rows, :], wq_ref[...], preferred_element_type=F32).astype(BF16).astype(F32)
    lane_head = iota((8, width), 1) // (width // heads)
    for g in range(rows // 8):
        piece = queries[8 * g : 8 * g + 8, :]
        qm_ref[g // groups, (g % groups) * lines : (g % groups + 1) * lines, :] = jnp.concatenate(
            [jnp.where(lane_head == h, piece, 0.0) for h in range(heads)], axis=0
        ).astype(BF16)


def pair_scores(
    mine_ref, first_ref, second_ref, qt_ref, qm_ref, k_ref, term_ref, f_ref, act_ref, s_ref, table_ref, heads
):
    blocks, rows, width = k_ref.shape
    spans = rows // SPAN
    groups = SPAN // 8
    lines = 8 * heads
    scale = LOG2E * (width // heads) ** (-0.5)

    ids = term_ref[7]
    least = jnp.min(ids, axis=1, keepdims=True)
    most = jnp.max(ids, axis=1, keepdims=True)
    weight = jnp.left_shift(1, iota((blocks, 1), 0)).astype(F32)
    q_ids = mine_ref[rows : rows + EXTRA, 0:rows].astype(F32)[4:5, :]
    lane = iota((1, rows), 1) // SPAN
    count = jnp.int32(0)
    for s in range(spans):
        q_least = jnp.min(jnp.where(lane == s, q_ids, 1e9), axis=1, keepdims=True)
        q_most = jnp.max(jnp.where(lane == s, q_ids, -1e9), axis=1, keepdims=True)
        live = (least <= q_most) & (most >= q_least)
        bits = jnp.sum(jnp.where(live, weight, 0.0)).astype(jnp.int32)
        for place in range(blocks):
            bit = lax.bitwise_and(lax.shift_right_logical(bits, place), 1)
            table_ref[count] = jnp.int32(16 * s + place)
            count = count + bit

            @pl.when(bit == 0)
            def blank(place=place, s=s):
                s_ref[place, s] = jnp.full((SPAN * heads, LANES), -1e30, F32)

    f_ref[96:128, :] = jnp.ones((32, groups * LANES), BF16)

    def features(s, j):
        k = [term_ref[t, pl.ds(j, 1), :] for t in range(7)]
        for g in range(groups):
            at = pl.multiple_of(s * SPAN + 8 * g, 8)
            q = [qt_ref[t, pl.ds(at, 8), :] for t in range(7)]
            gap = q[1] - k[1]
            cos_gap = q[2] * k[2] + q[3] * k[3]
            dist = gap * gap + (2.0 - cos_gap)
            low = jnp.minimum(q[0], k[0])
            pair_mass = (q[6] + k[6]) + (q[4] * k[5] + q[5] * k[4] - (q[0] * k[0]) * cos_gap)
            ab = jnp.concatenate([jnp.log2(1.0 + dist), jnp.log2(1.0 + low * low * dist)], axis=0)
            cd = jnp.concatenate([low / (q[0] + k[0]), jnp.log2(pair_mass)], axis=0)
            ab_hi, ab_lo = split(ab)
            cd_hi, cd_lo = split(cd)
            f_ref[0:96, g * LANES : (g + 1) * LANES] = jnp.concatenate(
                [ab_hi, cd_hi, ab_lo, cd_lo, ab_hi, cd_hi], axis=0
            )

    def score(s, j):
        bias2 = jnp.dot(second_ref[...], act_ref[...], preferred_element_type=F32)
        bias = bias2[0:lines, :] + bias2[lines:, :]
        match = lax.dot_general(
            qm_ref[s], k_ref[j], (((1,), (1,)), ((), ())), preferred_element_type=F32
        )
        key_ids = term_ref[7, pl.ds(j, 1), :]
        for g in range(groups):
            at = pl.multiple_of(s * SPAN + 8 * g, 8)
            live = qt_ref[7, pl.ds(at, 8), :] == key_ids
            for h in range(heads):
                line = g * lines + 8 * h
                value = match[line : line + 8, :] * scale + bias[8 * h : 8 * h + 8, g * LANES : (g + 1) * LANES]
                s_ref[j, s, line : line + 8, :] = jnp.where(live, value, -1e30)

    def task(at):
        code = table_ref[jnp.clip(at, 0, count - 1)]
        return lax.shift_right_logical(code, 4), lax.bitwise_and(code, 15)

    def step(at, carry):
        hidden = jnp.dot(first_ref[...], f_ref[...], preferred_element_type=F32)
        features(*task(at + 1))
        score(*task(at - 1))
        act = hidden * (1.0 + jnp.tanh(hidden * (hidden * hidden + BETA)))
        act_ref[...] = act.astype(BF16)
        return carry

    @pl.when(count > 0)
    def run():
        features(*task(0))
        lax.fori_loop(0, count, step, 0)
        score(*task(count - 1))


def own_kernel(mine_ref, wq_ref, wk_ref, wv_ref, first_ref, second_ref, s_ref, v_ref, qt_ref, qm_ref, *scratch, heads):
    x_ref, k_ref, raw_ref, term_ref, f_ref, act_ref, table_ref = scratch
    key_side([mine_ref], [None], wk_ref, wv_ref, x_ref, k_ref, v_ref, raw_ref, term_ref)
    query_side(mine_ref, wq_ref, term_ref, qt_ref, qm_ref, heads)
    pair_scores(
        mine_ref, first_ref, second_ref, qt_ref, qm_ref, k_ref, term_ref, f_ref, act_ref, s_ref, table_ref, heads
    )


def reaches(place, flip, blocks):
    return abs(place - (place ^ flip)) <= blocks // 2


def useful(flip, blocks):
    if not skips(flip, blocks):
        return None
    own = lax.axis_index("blk")
    return jnp.abs(own - lax.bitwise_xor(own, flip)) <= blocks // 2


def skips(flip, blocks):
    return blocks == 8 and not all(reaches(place, flip, blocks) for place in range(blocks))


def near_kernel(mine_ref, *refs, flips, blocks, heads):
    count = len(flips)
    got = refs[:count]
    wk_ref, wv_ref, first_ref, second_ref, qt_ref, qm_ref, s_ref, v_ref = refs[count : count + 8]
    x_ref, k_ref, raw_ref, term_ref, f_ref, act_ref, table_ref = refs[count + 8 :]
    checks = [useful(flip, blocks) for flip in flips]
    key_side(got, checks, wk_ref, wv_ref, x_ref, k_ref, v_ref, raw_ref, term_ref)
    pair_scores(
        mine_ref, first_ref, second_ref, qt_ref, qm_ref, k_ref, term_ref, f_ref, act_ref, s_ref, table_ref, heads
    )


def last_kernel(mine_ref, *refs, flips, blocks, heads):
    count = len(flips)
    got = refs[:count]
    wk_ref, wv_ref, first_ref, second_ref, qt_ref, qm_ref = refs[count : count + 6]
    s_own, s_near, v_own, v_near, wo_ref, gain_ref, out_ref = refs[count + 6 : count + 13]
    x_ref, k_ref, raw_ref, term_ref, f_ref, act_ref, table_ref, s_ref, v_ref, att_ref = refs[count + 13 :]
    checks = [useful(flip, blocks) for flip in flips]
    key_side(got, checks, wk_ref, wv_ref, x_ref, k_ref, v_ref, raw_ref, term_ref)
    pair_scores(
        mine_ref, first_ref, second_ref, qt_ref, qm_ref, k_ref, term_ref, f_ref, act_ref, s_ref, table_ref, heads
    )
    rows = out_ref.shape[0]
    width = out_ref.shape[1]
    lines = 8 * heads
    deep = (SPAN * heads, width)
    diag = (iota(deep, 0) % lines) // 8 == iota(deep, 1) // (width // heads)
    parts = [(s_own, v_own), (s_near, v_near), (s_ref, v_ref)]

    def attend(s, carry):
        top = None
        for scores, _ in parts:
            for j in range(scores.shape[0]):
                top = scores[j, s] if top is None else jnp.maximum(top, scores[j, s])
        top = jnp.max(top, axis=1, keepdims=True)
        total = jnp.zeros((SPAN * heads, LANES), F32)
        accum = jnp.zeros(deep, F32)
        for scores, values in parts:
            pieces = []
            for j in range(scores.shape[0]):
                weights = jnp.exp2(scores[j, s] - top)
                total = total + weights
                pieces.append(weights.astype(BF16))
            accum = accum + jnp.dot(
                jnp.concatenate(pieces, axis=1),
                values[...].reshape(len(pieces) * rows, width),
                preferred_element_type=F32,
            )
        total = jnp.sum(total, axis=1, keepdims=True)
        accum = jnp.where(diag, accum / total, 0.0)
        for g in range(SPAN // 8):
            out = accum[g * lines : g * lines + 8, :]
            for h in range(1, heads):
                out = out + accum[g * lines + 8 * h : g * lines + 8 * h + 8, :]
            att_ref[pl.ds(pl.multiple_of(s * SPAN + 8 * g, 8), 8), :] = out
        return carry

    lax.fori_loop(0, rows // SPAN, attend, 0)
    mixed = jnp.dot(att_ref[...].astype(BF16), wo_ref[...], preferred_element_type=F32)
    out_ref[...] = layer_norm(mixed, gain_ref[...]).astype(BF16)


def shards(
    raw,
    raw_kin,
    reader,
    event_id,
    pre_gain,
    w_query,
    w_key,
    w_value,
    w_out,
    post_gain,
    pair_w1,
    pair_b1,
    pair_w2,
):
    groups = raw.shape[1]
    rows = raw.shape[2]
    width = raw.shape[3]
    blocks = lax.axis_size("blk")
    heads = pair_w2.shape[1]
    hidden = pair_w1.shape[1]
    assert rows == LANES and blocks & (blocks - 1) == 0 and blocks <= 32
    raw = raw[0]
    raw_kin = raw_kin[0]
    array = jax.ShapeDtypeStruct
    message = array((rows + EXTRA, width), BF16)
    vmem = pl.BlockSpec(memory_space=pltpu.VMEM)
    hbm = pl.BlockSpec(memory_space=pltpu.HBM)

    def call(kernel, name, out_shape, operands, scratch=(), limit=8, specs=None):
        single = not isinstance(out_shape, list)
        return pl.pallas_call(
            kernel,
            out_shape=out_shape,
            in_specs=specs or [vmem] * len(operands),
            out_specs=vmem if single else [vmem] * len(out_shape),
            scratch_shapes=list(scratch),
            compiler_params=pltpu.CompilerParams(vmem_limit_bytes=limit * MIB),
            name=name,
        )(*[pltpu.with_memory_space_constraint(a, pltpu.HBM) for a in operands] if specs else operands)

    small = [reader, event_id, pre_gain[None], post_gain[None]]
    packed = call(
        pack_kernel,
        "pack",
        [message] * groups + [array(a.shape, a.dtype) for a in small],
        [raw, raw_kin, *small],
        [pltpu.VMEM(raw_kin.shape, BF16), pltpu.SemaphoreType.DMA((groups + 5,))],
        specs=[hbm] * 6,
    )
    reader, event_id, pre_row, post_row = packed[groups:]
    parts = [packed[0]] + [
        lax.ppermute(packed[s], "grp", [(i, (i + s) % groups) for i in range(groups)])
        for s in range(1, groups)
    ]
    local = [pair_w1, pair_b1[None], pair_w2.T]
    dense = [w_query, w_key, w_value, w_out]
    w_query, w_key, w_value, w_out, first, second = call(
        weights_kernel,
        "weights",
        [array(a.shape, a.dtype) for a in dense]
        + [array((8 * hidden, LANES), BF16), array((16 * heads, 8 * hidden), BF16)],
        local + dense,
        [pltpu.VMEM(a.shape, a.dtype) for a in local] + [pltpu.SemaphoreType.DMA((7,))],
        specs=[hbm] * 7,
    )
    mine = call(choose_kernel, "choose", message, [reader, event_id, pre_row, first, *parts])

    soon = [1, 2, 6, 7] if blocks == 8 else list(range(1, blocks, 2))
    late = [flip for flip in range(1, blocks) if flip not in soon]
    messages = {}
    for flip in soon + late:
        pairs = [(i, i ^ flip) for i in range(blocks)]
        if skips(flip, blocks):
            pairs = [(i, i ^ flip if reaches(i, flip, blocks) else i) for i in range(blocks)]
        messages[flip] = lax.ppermute(mine, "blk", pairs)

    spans = rows // SPAN
    lanes = SPAN // 8 * LANES
    tall = SPAN * heads

    def scratch(count):
        return [
            pltpu.VMEM((count, rows, width), BF16),
            pltpu.VMEM((count, rows, width), BF16),
            pltpu.VMEM((5, count, rows), F32),
            pltpu.VMEM((8, count, rows), F32),
            pltpu.VMEM((LANES, lanes), BF16),
            pltpu.VMEM((8 * hidden, lanes), BF16),
            pltpu.SMEM((spans * count + 1,), jnp.int32),
        ]

    def results(count):
        return [array((count, spans, tall, LANES), F32), array((count, rows, width), BF16)]

    s_own, v_own, q_terms, q_heads = call(
        lambda *refs: own_kernel(*refs, heads=heads),
        "own",
        results(1) + [array((8, rows, LANES), F32), array((spans, tall, width), BF16)],
        [mine, w_query, w_key, w_value, first, second],
        scratch(1),
        limit=10,
    )
    s_near, v_near = call(
        lambda *refs: near_kernel(*refs, flips=soon, blocks=blocks, heads=heads),
        "near",
        results(len(soon)),
        [mine, *[messages[flip] for flip in soon], w_key, w_value, first, second, q_terms, q_heads],
        scratch(len(soon)),
        limit=12 + blocks // 2,
    )
    far_scratch = scratch(len(late))
    far_shapes = [
        pltpu.VMEM((len(late), spans, tall, LANES), F32),
        pltpu.VMEM((len(late), rows, width), BF16),
        pltpu.VMEM((rows, width), F32),
    ]
    encoded = call(
        lambda *refs: last_kernel(*refs, flips=late, blocks=blocks, heads=heads),
        "last",
        array((rows, width), BF16),
        [mine, *[messages[flip] for flip in late], w_key, w_value, first, second, q_terms, q_heads]
        + [s_own, s_near, v_own, v_near, w_out, post_row],
        far_scratch + far_shapes,
        limit=14 + 3 * blocks // 2,
    )
    return encoded[None]


def solution(mesh):
    in_specs = (
        P("grp", None, "blk", None),
        P("grp", None, None, "blk"),
        P("grp", "blk"),
        P("grp", "blk"),
        P(),
        P(),
        P(),
        P(),
        P(),
        P(),
        P(),
        P(),
        P(),
    )
    out_specs = P("grp", "blk", None)
    return jax.shard_map(shards, mesh=mesh, in_specs=in_specs, out_specs=out_specs, check_vma=False)
```

```python
import math

import jax
import jax.numpy as jnp
from jax import lax
from jax.experimental import pallas as pl
from jax.experimental.pallas import tpu as pltpu
from jax.sharding import PartitionSpec as P


F32 = jnp.float32
BF16 = jnp.bfloat16
EXTRA = 16
LANES = 128
SPAN = 32
MIB = 1 << 20

SQ = math.sqrt(2.0 / math.pi)
GAMMA = (SQ * 0.044715) ** (1.0 / 3.0)
BETA = SQ / GAMMA
LOG2E = math.log2(math.e)
LN2 = math.log(2.0)


def iota(shape, axis):
    return lax.broadcasted_iota(jnp.int32, shape, axis)


def layer_norm(rows, gain):
    center = rows - jnp.mean(rows, axis=-1, keepdims=True)
    spread = jnp.mean(center * center, axis=-1, keepdims=True)
    return center * lax.rsqrt(spread + 1e-05) * gain


def pack_kernel(raw_ref, kin_ref, reader_ref, ids_ref, pre_ref, post_ref, *refs):
    groups, rows, width = raw_ref.shape
    messages = refs[:groups]
    copies = refs[groups : groups + 4]
    kin_own, sems = refs[groups + 4 :]
    own = lax.axis_index("grp")
    moves = [
        pltpu.make_async_copy(raw_ref.at[lax.rem(own + step, groups)], out.at[pl.ds(0, rows)], sems.at[step])
        for step, out in enumerate(messages)
    ]
    first = pltpu.make_async_copy(kin_ref, kin_own, sems.at[groups])
    first.start()
    for move in moves:
        move.start()
    others = [
        pltpu.make_async_copy(source, out, sems.at[groups + 1 + at])
        for at, (source, out) in enumerate(zip((reader_ref, ids_ref, pre_ref, post_ref), copies))
    ]
    for move in others:
        move.start()
    first.wait()
    for step, out in enumerate(messages):
        kin = kin_own[lax.rem(own + step, groups)]
        out[rows : rows + EXTRA, :] = jnp.concatenate(
            [
                jnp.concatenate([kin, jnp.zeros((4, width - rows), BF16)], axis=1),
                jnp.zeros((EXTRA - 4, width), BF16),
            ],
            axis=0,
        )
    for move in moves + others:
        move.wait()


def choose_kernel(reader_ref, ids_ref, gain_ref, ready_ref, *refs):
    got = refs[:-1]
    out = refs[-1]
    groups = len(got)
    rows = got[0].shape[0] - EXTRA
    width = got[0].shape[1]
    own = lax.axis_index("grp")
    by_lane = reader_ref[...].astype(F32)
    by_row = jnp.transpose(jnp.broadcast_to(by_lane, (LANES, rows)))
    by_row = jnp.concatenate([by_row] * (width // LANES), axis=1)
    tokens = jnp.zeros((rows, width), F32)
    kin = jnp.zeros((4, rows), F32)
    for step, ref in enumerate(got):
        source = lax.rem(own + groups - step, groups).astype(F32)
        tokens = jnp.where(by_row == source, ref[0:rows, :].astype(F32), tokens)
        kin = jnp.where(by_lane == source, ref[rows : rows + EXTRA, 0:rows].astype(F32)[0:4], kin)
    out[0:rows, :] = layer_norm(tokens, gain_ref[...]).astype(BF16)
    block = jnp.concatenate([kin, ids_ref[...].astype(F32), jnp.zeros((EXTRA - 5, rows), F32)], axis=0)
    block = jnp.concatenate([block, jnp.zeros((EXTRA, width - rows), F32)], axis=1)
    out[rows : rows + EXTRA, :] = block.astype(BF16)


def split(value):
    high = value.astype(BF16)
    return high, (value - high.astype(F32)).astype(BF16)


def weights_kernel(*refs):
    sources = refs[:7]
    copies = refs[7:11]
    first_ref, second_ref, w1_ref, b1_ref, w2_ref, sems = refs[11:]
    moves = [
        pltpu.make_async_copy(source, out, sems.at[at])
        for at, (source, out) in enumerate(zip(sources, (w1_ref, b1_ref, w2_ref, *copies)))
    ]
    for move in moves:
        move.start()
    for move in moves[:3]:
        move.wait()
    hidden = w1_ref.shape[1]
    heads = w2_ref.shape[0]
    row = lax.broadcasted_iota(jnp.int32, (4, hidden), 0)
    w1 = w1_ref[...] * jnp.where(row == 2, GAMMA, GAMMA * LN2)
    w1_hi, w1_lo = split(w1)
    b1 = b1_ref[...] * GAMMA
    b_hi, b_mid = split(b1)
    b_lo = b1 - b_hi.astype(F32) - b_mid.astype(F32)
    stack = jnp.concatenate(
        [
            w1_hi.astype(F32),
            w1_lo.astype(F32),
            b_hi.astype(F32),
            b_mid.astype(F32),
            b_lo,
            jnp.zeros((5, hidden), F32),
        ],
        axis=0,
    ).astype(BF16)

    def onehot(hit):
        return jnp.where(hit, 1.0, 0.0).astype(BF16)

    units = hidden * 8
    grown = onehot(iota((hidden, units), 1) // 8 == iota((hidden, units), 0))
    tall = jnp.dot(stack, grown, preferred_element_type=F32).astype(BF16)
    col = iota((16, LANES), 1)
    which = jnp.where(col < 32, col // 8, jnp.where(col < 96, col // 8 - 4, col - 88))
    pick = onehot((which == iota((16, LANES), 0)) & (col < 99))
    first = lax.dot_general(tall, pick, (((0,), (0,)), ((), ())), preferred_element_type=F32)
    col = iota((units, LANES), 1)
    same = (iota((units, LANES), 0) % 8 == col % 8) | (col >= 96)
    first_ref[...] = jnp.where(same, first, 0.0).astype(BF16)

    w2_hi, w2_lo = split(w2_ref[...] * (LOG2E * 0.5 / GAMMA))
    wide = [jnp.dot(w, grown, preferred_element_type=F32) for w in (w2_hi, w2_lo)]
    wide = jnp.concatenate(wide, axis=0).astype(BF16)
    shape = (16 * heads, 2 * heads)
    lift = onehot(iota(shape, 0) // 8 == iota(shape, 1))
    second = jnp.dot(lift, wide, preferred_element_type=F32)
    shape = (16 * heads, units)
    second_ref[...] = jnp.where(iota(shape, 0) % 8 == iota(shape, 1) % 8, second, 0.0).astype(BF16)
    for move in moves[3:]:
        move.wait()


def key_side(got, checks, wk_ref, wv_ref, x_ref, k_ref, v_ref, raw_ref, term_ref):
    count = len(got)
    rows = got[0].shape[0] - EXTRA
    width = got[0].shape[1]
    for place, (ref, check) in enumerate(zip(got, checks)):
        x_ref[place] = ref[0:rows, :]
        extra = ref[rows : rows + EXTRA, 0:rows].astype(F32)
        for row in range(4):
            raw_ref[row, place : place + 1, :] = extra[row : row + 1, :]
        event = extra[4:5, :]
        raw_ref[4, place : place + 1, :] = event if check is None else jnp.where(check, event, -1.0)
    feats = x_ref[...].reshape(count * rows, width)
    shape = (count, rows, width)
    k_ref[...] = jnp.dot(feats, wk_ref[...], preferred_element_type=F32).astype(BF16).reshape(shape)
    v_ref[...] = jnp.dot(feats, wv_ref[...], preferred_element_type=F32).astype(BF16).reshape(shape)
    pt = raw_ref[0]
    rap = raw_ref[1]
    phi = raw_ref[2]
    mass = raw_ref[3]
    m2 = mass * mass
    mt = jnp.sqrt(pt * pt + m2)
    terms = (pt, rap, jnp.cos(phi), jnp.sin(phi), mt * jnp.exp(rap), mt * jnp.exp(-rap), m2, raw_ref[4])
    for t, term in enumerate(terms):
        term_ref[t] = term


def query_side(mine_ref, wq_ref, term_ref, qt_ref, qm_ref, heads):
    rows = mine_ref.shape[0] - EXTRA
    width = mine_ref.shape[1]
    groups = SPAN // 8
    lines = 8 * heads
    mine = jnp.concatenate([term_ref[t, 0:1, :] for t in range(8)], axis=0)
    factor = iota((8, rows), 0)
    scaled = jnp.where((factor == 2) | (factor == 3), mine * 2.0, mine)
    scaled = jnp.where(factor == 6, mine + 1.0, scaled)
    cols = jnp.transpose(jnp.concatenate([scaled, jnp.zeros((LANES - 8, rows), F32)], axis=0))
    for t in range(8):
        qt_ref[t] = jnp.broadcast_to(cols[:, t : t + 1], (rows, LANES))
    queries = jnp.dot(mine_ref[0:rows, :], wq_ref[...], preferred_element_type=F32).astype(BF16).astype(F32)
    lane_head = iota((8, width), 1) // (width // heads)
    for g in range(rows // 8):
        piece = queries[8 * g : 8 * g + 8, :]
        qm_ref[g // groups, (g % groups) * lines : (g % groups + 1) * lines, :] = jnp.concatenate(
            [jnp.where(lane_head == h, piece, 0.0) for h in range(heads)], axis=0
        ).astype(BF16)


def pair_scores(
    mine_ref, first_ref, second_ref, qt_ref, qm_ref, k_ref, term_ref, f_ref, act_ref, s_ref, table_ref, heads
):
    blocks, rows, width = k_ref.shape
    spans = rows // SPAN
    groups = SPAN // 8
    lines = 8 * heads
    scale = LOG2E * (width // heads) ** (-0.5)

    ids = term_ref[7]
    least = jnp.min(ids, axis=1, keepdims=True)
    most = jnp.max(ids, axis=1, keepdims=True)
    weight = jnp.left_shift(1, iota((blocks, 1), 0)).astype(F32)
    q_ids = mine_ref[rows : rows + EXTRA, 0:rows].astype(F32)[4:5, :]
    lane = iota((1, rows), 1) // SPAN
    count = jnp.int32(0)
    for s in range(spans):
        q_least = jnp.min(jnp.where(lane == s, q_ids, 1e9), axis=1, keepdims=True)
        q_most = jnp.max(jnp.where(lane == s, q_ids, -1e9), axis=1, keepdims=True)
        live = (least <= q_most) & (most >= q_least)
        bits = jnp.sum(jnp.where(live, weight, 0.0)).astype(jnp.int32)
        for place in range(blocks):
            bit = lax.bitwise_and(lax.shift_right_logical(bits, place), 1)
            table_ref[count] = jnp.int32(16 * s + place)
            count = count + bit

            @pl.when(bit == 0)
            def blank(place=place, s=s):
                s_ref[place, s] = jnp.full((SPAN * heads, LANES), -1e30, F32)

    f_ref[96:128, :] = jnp.ones((32, groups * LANES), BF16)

    def features(s, j):
        k = [term_ref[t, pl.ds(j, 1), :] for t in range(7)]
        for g in range(groups):
            at = pl.multiple_of(s * SPAN + 8 * g, 8)
            q = [qt_ref[t, pl.ds(at, 8), :] for t in range(7)]
            gap = q[1] - k[1]
            cos_gap = q[2] * k[2] + q[3] * k[3]
            dist = gap * gap + (2.0 - cos_gap)
            low = jnp.minimum(q[0], k[0])
            pair_mass = (q[6] + k[6]) + (q[4] * k[5] + q[5] * k[4] - (q[0] * k[0]) * cos_gap)
            ab = jnp.concatenate([jnp.log2(1.0 + dist), jnp.log2(1.0 + low * low * dist)], axis=0)
            cd = jnp.concatenate([low / (q[0] + k[0]), jnp.log2(pair_mass)], axis=0)
            ab_hi, ab_lo = split(ab)
            cd_hi, cd_lo = split(cd)
            f_ref[0:96, g * LANES : (g + 1) * LANES] = jnp.concatenate(
                [ab_hi, cd_hi, ab_lo, cd_lo, ab_hi, cd_hi], axis=0
            )

    def score(s, j):
        bias2 = jnp.dot(second_ref[...], act_ref[...], preferred_element_type=F32)
        bias = bias2[0:lines, :] + bias2[lines:, :]
        match = lax.dot_general(
            qm_ref[s], k_ref[j], (((1,), (1,)), ((), ())), preferred_element_type=F32
        )
        key_ids = term_ref[7, pl.ds(j, 1), :]
        for g in range(groups):
            at = pl.multiple_of(s * SPAN + 8 * g, 8)
            live = qt_ref[7, pl.ds(at, 8), :] == key_ids
            for h in range(heads):
                line = g * lines + 8 * h
                value = match[line : line + 8, :] * scale + bias[8 * h : 8 * h + 8, g * LANES : (g + 1) * LANES]
                s_ref[j, s, line : line + 8, :] = jnp.where(live, value, -1e30)

    def task(at):
        code = table_ref[jnp.clip(at, 0, count - 1)]
        return lax.shift_right_logical(code, 4), lax.bitwise_and(code, 15)

    def step(at, carry):
        hidden = jnp.dot(first_ref[...], f_ref[...], preferred_element_type=F32)
        features(*task(at + 1))
        score(*task(at - 1))
        act = hidden * (1.0 + jnp.tanh(hidden * (hidden * hidden + BETA)))
        act_ref[...] = act.astype(BF16)
        return carry

    @pl.when(count > 0)
    def run():
        features(*task(0))
        lax.fori_loop(0, count, step, 0)
        score(*task(count - 1))


def own_kernel(mine_ref, wq_ref, wk_ref, wv_ref, first_ref, second_ref, s_ref, v_ref, qt_ref, qm_ref, *scratch, heads):
    x_ref, k_ref, raw_ref, term_ref, f_ref, act_ref, table_ref = scratch
    key_side([mine_ref], [None], wk_ref, wv_ref, x_ref, k_ref, v_ref, raw_ref, term_ref)
    query_side(mine_ref, wq_ref, term_ref, qt_ref, qm_ref, heads)
    pair_scores(
        mine_ref, first_ref, second_ref, qt_ref, qm_ref, k_ref, term_ref, f_ref, act_ref, s_ref, table_ref, heads
    )


def reaches(place, flip, blocks):
    return abs(place - (place ^ flip)) <= blocks // 2


def useful(flip, blocks):
    if not skips(flip, blocks):
        return None
    own = lax.axis_index("blk")
    return jnp.abs(own - lax.bitwise_xor(own, flip)) <= blocks // 2


def skips(flip, blocks):
    return blocks == 8 and not all(reaches(place, flip, blocks) for place in range(blocks))


def near_kernel(mine_ref, *refs, flips, blocks, heads):
    count = len(flips)
    got = refs[:count]
    wk_ref, wv_ref, first_ref, second_ref, qt_ref, qm_ref, s_ref, v_ref = refs[count : count + 8]
    x_ref, k_ref, raw_ref, term_ref, f_ref, act_ref, table_ref = refs[count + 8 :]
    checks = [useful(flip, blocks) for flip in flips]
    key_side(got, checks, wk_ref, wv_ref, x_ref, k_ref, v_ref, raw_ref, term_ref)
    pair_scores(
        mine_ref, first_ref, second_ref, qt_ref, qm_ref, k_ref, term_ref, f_ref, act_ref, s_ref, table_ref, heads
    )


def last_kernel(mine_ref, *refs, flips, blocks, heads):
    count = len(flips)
    got = refs[:count]
    wk_ref, wv_ref, first_ref, second_ref, qt_ref, qm_ref = refs[count : count + 6]
    s_own, s_near, v_own, v_near, wo_ref, gain_ref, out_ref = refs[count + 6 : count + 13]
    x_ref, k_ref, raw_ref, term_ref, f_ref, act_ref, table_ref, s_ref, v_ref, att_ref = refs[count + 13 :]
    checks = [useful(flip, blocks) for flip in flips]
    key_side(got, checks, wk_ref, wv_ref, x_ref, k_ref, v_ref, raw_ref, term_ref)
    pair_scores(
        mine_ref, first_ref, second_ref, qt_ref, qm_ref, k_ref, term_ref, f_ref, act_ref, s_ref, table_ref, heads
    )
    rows = out_ref.shape[0]
    width = out_ref.shape[1]
    lines = 8 * heads
    deep = (SPAN * heads, width)
    diag = (iota(deep, 0) % lines) // 8 == iota(deep, 1) // (width // heads)
    parts = [(s_own, v_own), (s_near, v_near), (s_ref, v_ref)]

    def attend(s, carry):
        top = None
        for scores, _ in parts:
            for j in range(scores.shape[0]):
                top = scores[j, s] if top is None else jnp.maximum(top, scores[j, s])
        top = jnp.max(top, axis=1, keepdims=True)
        total = jnp.zeros((SPAN * heads, LANES), F32)
        accum = jnp.zeros(deep, F32)
        for scores, values in parts:
            pieces = []
            for j in range(scores.shape[0]):
                weights = jnp.exp2(scores[j, s] - top)
                total = total + weights
                pieces.append(weights.astype(BF16))
            accum = accum + jnp.dot(
                jnp.concatenate(pieces, axis=1),
                values[...].reshape(len(pieces) * rows, width),
                preferred_element_type=F32,
            )
        total = jnp.sum(total, axis=1, keepdims=True)
        accum = jnp.where(diag, accum / total, 0.0)
        for g in range(SPAN // 8):
            out = accum[g * lines : g * lines + 8, :]
            for h in range(1, heads):
                out = out + accum[g * lines + 8 * h : g * lines + 8 * h + 8, :]
            att_ref[pl.ds(pl.multiple_of(s * SPAN + 8 * g, 8), 8), :] = out
        return carry

    lax.fori_loop(0, rows // SPAN, attend, 0)
    mixed = jnp.dot(att_ref[...].astype(BF16), wo_ref[...], preferred_element_type=F32)
    out_ref[...] = layer_norm(mixed, gain_ref[...]).astype(BF16)


def shards(
    raw,
    raw_kin,
    reader,
    event_id,
    pre_gain,
    w_query,
    w_key,
    w_value,
    w_out,
    post_gain,
    pair_w1,
    pair_b1,
    pair_w2,
):
    groups = raw.shape[1]
    rows = raw.shape[2]
    width = raw.shape[3]
    blocks = lax.axis_size("blk")
    heads = pair_w2.shape[1]
    hidden = pair_w1.shape[1]
    assert rows == LANES and blocks & (blocks - 1) == 0 and blocks <= 32
    raw = raw[0]
    raw_kin = raw_kin[0]
    array = jax.ShapeDtypeStruct
    message = array((rows + EXTRA, width), BF16)
    vmem = pl.BlockSpec(memory_space=pltpu.VMEM)
    hbm = pl.BlockSpec(memory_space=pltpu.HBM)

    def call(kernel, name, out_shape, operands, scratch=(), limit=8, specs=None):
        single = not isinstance(out_shape, list)
        return pl.pallas_call(
            kernel,
            out_shape=out_shape,
            in_specs=specs or [vmem] * len(operands),
            out_specs=vmem if single else [vmem] * len(out_shape),
            scratch_shapes=list(scratch),
            compiler_params=pltpu.CompilerParams(vmem_limit_bytes=limit * MIB),
            name=name,
        )(*[pltpu.with_memory_space_constraint(a, pltpu.HBM) for a in operands] if specs else operands)

    small = [reader, event_id, pre_gain[None], post_gain[None]]
    packed = call(
        pack_kernel,
        "pack",
        [message] * groups + [array(a.shape, a.dtype) for a in small],
        [raw, raw_kin, *small],
        [pltpu.VMEM(raw_kin.shape, BF16), pltpu.SemaphoreType.DMA((groups + 5,))],
        specs=[hbm] * 6,
    )
    reader, event_id, pre_row, post_row = packed[groups:]
    parts = [packed[0]] + [
        lax.ppermute(packed[s], "grp", [(i, (i + s) % groups) for i in range(groups)])
        for s in range(1, groups)
    ]
    local = [pair_w1, pair_b1[None], pair_w2.T]
    dense = [w_query, w_key, w_value, w_out]
    w_query, w_key, w_value, w_out, first, second = call(
        weights_kernel,
        "weights",
        [array(a.shape, a.dtype) for a in dense]
        + [array((8 * hidden, LANES), BF16), array((16 * heads, 8 * hidden), BF16)],
        local + dense,
        [pltpu.VMEM(a.shape, a.dtype) for a in local] + [pltpu.SemaphoreType.DMA((7,))],
        specs=[hbm] * 7,
    )
    mine = call(choose_kernel, "choose", message, [reader, event_id, pre_row, first, *parts])

    soon = [1, 2, 3] if blocks == 8 else list(range(1, blocks, 2))
    late = [6, 7, 4, 5] if blocks == 8 else list(range(2, blocks, 2))

    def swap(part, flip):
        pairs = [(i, i ^ flip) for i in range(blocks)]
        if skips(flip, blocks):
            pairs = [(i, i ^ flip if reaches(i, flip, blocks) else i) for i in range(blocks)]
        return lax.ppermute(part, "blk", pairs)

    messages = {flip: swap(mine, flip) for flip in soon}

    spans = rows // SPAN
    lanes = SPAN // 8 * LANES
    tall = SPAN * heads

    def scratch(count):
        return [
            pltpu.VMEM((count, rows, width), BF16),
            pltpu.VMEM((count, rows, width), BF16),
            pltpu.VMEM((5, count, rows), F32),
            pltpu.VMEM((8, count, rows), F32),
            pltpu.VMEM((LANES, lanes), BF16),
            pltpu.VMEM((8 * hidden, lanes), BF16),
            pltpu.SMEM((spans * count + 1,), jnp.int32),
        ]

    def results(count):
        return [array((count, spans, tall, LANES), F32), array((count, rows, width), BF16)]

    s_own, v_own, q_terms, q_heads = call(
        lambda *refs: own_kernel(*refs, heads=heads),
        "own",
        results(1) + [array((8, rows, LANES), F32), array((spans, tall, width), BF16)],
        [mine, w_query, w_key, w_value, first, second],
        scratch(1),
        limit=10,
    )
    held, q_terms = lax.optimization_barrier((mine, q_terms))
    messages.update({flip: swap(held, flip) for flip in late})
    s_near, v_near = call(
        lambda *refs: near_kernel(*refs, flips=soon, blocks=blocks, heads=heads),
        "near",
        results(len(soon)),
        [mine, *[messages[flip] for flip in soon], w_key, w_value, first, second, q_terms, q_heads],
        scratch(len(soon)),
        limit=12 + blocks // 2,
    )
    far_scratch = scratch(len(late))
    far_shapes = [
        pltpu.VMEM((len(late), spans, tall, LANES), F32),
        pltpu.VMEM((len(late), rows, width), BF16),
        pltpu.VMEM((rows, width), F32),
    ]
    encoded = call(
        lambda *refs: last_kernel(*refs, flips=late, blocks=blocks, heads=heads),
        "last",
        array((rows, width), BF16),
        [mine, *[messages[flip] for flip in late], w_key, w_value, first, second, q_terms, q_heads]
        + [s_own, s_near, v_own, v_near, w_out, post_row],
        far_scratch + far_shapes,
        limit=14 + 3 * blocks // 2,
    )
    return encoded[None]


def solution(mesh):
    in_specs = (
        P("grp", None, "blk", None),
        P("grp", None, None, "blk"),
        P("grp", "blk"),
        P("grp", "blk"),
        P(),
        P(),
        P(),
        P(),
        P(),
        P(),
        P(),
        P(),
        P(),
    )
    out_specs = P("grp", "blk", None)
    return jax.shard_map(shards, mesh=mesh, in_specs=in_specs, out_specs=out_specs, check_vma=False)
```

```python
import math

import jax
import jax.numpy as jnp
from jax import lax
from jax.experimental import pallas as pl
from jax.experimental.pallas import tpu as pltpu
from jax.sharding import PartitionSpec as P


F32 = jnp.float32
BF16 = jnp.bfloat16
EXTRA = 16
LANES = 128
SPAN = 32
MIB = 1 << 20

SQ = math.sqrt(2.0 / math.pi)
GAMMA = (SQ * 0.044715) ** (1.0 / 3.0)
BETA = SQ / GAMMA
LOG2E = math.log2(math.e)
LN2 = math.log(2.0)


def iota(shape, axis):
    return lax.broadcasted_iota(jnp.int32, shape, axis)


def layer_norm(rows, gain):
    center = rows - jnp.mean(rows, axis=-1, keepdims=True)
    spread = jnp.mean(center * center, axis=-1, keepdims=True)
    return center * lax.rsqrt(spread + 1e-05) * gain


def pack_kernel(raw_ref, kin_ref, reader_ref, ids_ref, pre_ref, post_ref, *refs):
    groups, rows, width = raw_ref.shape
    messages = refs[:groups]
    copies = refs[groups : groups + 4]
    kin_own, sems = refs[groups + 4 :]
    own = lax.axis_index("grp")
    moves = [
        pltpu.make_async_copy(raw_ref.at[lax.rem(own + step, groups)], out.at[pl.ds(0, rows)], sems.at[step])
        for step, out in enumerate(messages)
    ]
    first = pltpu.make_async_copy(kin_ref, kin_own, sems.at[groups])
    first.start()
    for move in moves:
        move.start()
    others = [
        pltpu.make_async_copy(source, out, sems.at[groups + 1 + at])
        for at, (source, out) in enumerate(zip((reader_ref, ids_ref, pre_ref, post_ref), copies))
    ]
    for move in others:
        move.start()
    first.wait()
    for step, out in enumerate(messages):
        kin = kin_own[lax.rem(own + step, groups)]
        out[rows : rows + EXTRA, :] = jnp.concatenate(
            [
                jnp.concatenate([kin, jnp.zeros((4, width - rows), BF16)], axis=1),
                jnp.zeros((EXTRA - 4, width), BF16),
            ],
            axis=0,
        )
    for move in moves + others:
        move.wait()


def choose_kernel(reader_ref, ids_ref, gain_ref, ready_ref, *refs):
    got = refs[:-1]
    out = refs[-1]
    groups = len(got)
    rows = got[0].shape[0] - EXTRA
    width = got[0].shape[1]
    own = lax.axis_index("grp")
    by_lane = reader_ref[...].astype(F32)
    by_row = jnp.transpose(jnp.broadcast_to(by_lane, (LANES, rows)))
    by_row = jnp.concatenate([by_row] * (width // LANES), axis=1)
    tokens = jnp.zeros((rows, width), F32)
    kin = jnp.zeros((4, rows), F32)
    for step, ref in enumerate(got):
        source = lax.rem(own + groups - step, groups).astype(F32)
        tokens = jnp.where(by_row == source, ref[0:rows, :].astype(F32), tokens)
        kin = jnp.where(by_lane == source, ref[rows : rows + EXTRA, 0:rows].astype(F32)[0:4], kin)
    out[0:rows, :] = layer_norm(tokens, gain_ref[...]).astype(BF16)
    block = jnp.concatenate([kin, ids_ref[...].astype(F32), jnp.zeros((EXTRA - 5, rows), F32)], axis=0)
    block = jnp.concatenate([block, jnp.zeros((EXTRA, width - rows), F32)], axis=1)
    out[rows : rows + EXTRA, :] = block.astype(BF16)


def split(value):
    high = value.astype(BF16)
    return high, (value - high.astype(F32)).astype(BF16)


def weights_kernel(*refs):
    sources = refs[:7]
    copies = refs[7:11]
    first_ref, second_ref, w1_ref, b1_ref, w2_ref, sems = refs[11:]
    moves = [
        pltpu.make_async_copy(source, out, sems.at[at])
        for at, (source, out) in enumerate(zip(sources, (w1_ref, b1_ref, w2_ref, *copies)))
    ]
    for move in moves:
        move.start()
    for move in moves[:3]:
        move.wait()
    hidden = w1_ref.shape[1]
    heads = w2_ref.shape[0]
    row = lax.broadcasted_iota(jnp.int32, (4, hidden), 0)
    w1 = w1_ref[...] * jnp.where(row == 2, GAMMA, GAMMA * LN2)
    w1_hi, w1_lo = split(w1)
    b1 = b1_ref[...] * GAMMA
    b_hi, b_mid = split(b1)
    b_lo = b1 - b_hi.astype(F32) - b_mid.astype(F32)
    stack = jnp.concatenate(
        [
            w1_hi.astype(F32),
            w1_lo.astype(F32),
            b_hi.astype(F32),
            b_mid.astype(F32),
            b_lo,
            jnp.zeros((5, hidden), F32),
        ],
        axis=0,
    ).astype(BF16)

    def onehot(hit):
        return jnp.where(hit, 1.0, 0.0).astype(BF16)

    units = hidden * 8
    grown = onehot(iota((hidden, units), 1) // 8 == iota((hidden, units), 0))
    tall = jnp.dot(stack, grown, preferred_element_type=F32).astype(BF16)
    col = iota((16, LANES), 1)
    which = jnp.where(col < 32, col // 8, jnp.where(col < 96, col // 8 - 4, col - 88))
    pick = onehot((which == iota((16, LANES), 0)) & (col < 99))
    first = lax.dot_general(tall, pick, (((0,), (0,)), ((), ())), preferred_element_type=F32)
    col = iota((units, LANES), 1)
    same = (iota((units, LANES), 0) % 8 == col % 8) | (col >= 96)
    first_ref[...] = jnp.where(same, first, 0.0).astype(BF16)

    w2_hi, w2_lo = split(w2_ref[...] * (LOG2E * 0.5 / GAMMA))
    wide = [jnp.dot(w, grown, preferred_element_type=F32) for w in (w2_hi, w2_lo)]
    wide = jnp.concatenate(wide, axis=0).astype(BF16)
    shape = (16 * heads, 2 * heads)
    lift = onehot(iota(shape, 0) // 8 == iota(shape, 1))
    second = jnp.dot(lift, wide, preferred_element_type=F32)
    shape = (16 * heads, units)
    second_ref[...] = jnp.where(iota(shape, 0) % 8 == iota(shape, 1) % 8, second, 0.0).astype(BF16)
    for move in moves[3:]:
        move.wait()


def key_side(got, checks, wk_ref, wv_ref, x_ref, k_ref, v_ref, raw_ref, term_ref):
    count = len(got)
    rows = got[0].shape[0] - EXTRA
    width = got[0].shape[1]
    for place, (ref, check) in enumerate(zip(got, checks)):
        x_ref[place] = ref[0:rows, :]
        extra = ref[rows : rows + EXTRA, 0:rows].astype(F32)
        for row in range(4):
            raw_ref[row, place : place + 1, :] = extra[row : row + 1, :]
        event = extra[4:5, :]
        raw_ref[4, place : place + 1, :] = event if check is None else jnp.where(check, event, -1.0)
    feats = x_ref[...].reshape(count * rows, width)
    shape = (count, rows, width)
    k_ref[...] = jnp.dot(feats, wk_ref[...], preferred_element_type=F32).astype(BF16).reshape(shape)
    v_ref[...] = jnp.dot(feats, wv_ref[...], preferred_element_type=F32).astype(BF16).reshape(shape)
    pt = raw_ref[0]
    rap = raw_ref[1]
    phi = raw_ref[2]
    mass = raw_ref[3]
    m2 = mass * mass
    mt = jnp.sqrt(pt * pt + m2)
    terms = (pt, rap, jnp.cos(phi), jnp.sin(phi), mt * jnp.exp(rap), mt * jnp.exp(-rap), m2, raw_ref[4])
    for t, term in enumerate(terms):
        term_ref[t] = term


def query_side(mine_ref, wq_ref, term_ref, qt_ref, qm_ref, heads):
    rows = mine_ref.shape[0] - EXTRA
    width = mine_ref.shape[1]
    groups = SPAN // 8
    lines = 8 * heads
    mine = jnp.concatenate([term_ref[t, 0:1, :] for t in range(8)], axis=0)
    factor = iota((8, rows), 0)
    scaled = jnp.where((factor == 2) | (factor == 3), mine * 2.0, mine)
    scaled = jnp.where(factor == 6, mine + 1.0, scaled)
    cols = jnp.transpose(jnp.concatenate([scaled, jnp.zeros((LANES - 8, rows), F32)], axis=0))
    for t in range(8):
        qt_ref[t] = jnp.broadcast_to(cols[:, t : t + 1], (rows, LANES))
    queries = jnp.dot(mine_ref[0:rows, :], wq_ref[...], preferred_element_type=F32).astype(BF16).astype(F32)
    lane_head = iota((8, width), 1) // (width // heads)
    for g in range(rows // 8):
        piece = queries[8 * g : 8 * g + 8, :]
        qm_ref[g // groups, (g % groups) * lines : (g % groups + 1) * lines, :] = jnp.concatenate(
            [jnp.where(lane_head == h, piece, 0.0) for h in range(heads)], axis=0
        ).astype(BF16)


def pair_scores(
    mine_ref, first_ref, second_ref, qt_ref, qm_ref, k_ref, term_ref, f_ref, act_ref, s_ref, table_ref, heads
):
    blocks, rows, width = k_ref.shape
    spans = rows // SPAN
    groups = SPAN // 8
    lines = 8 * heads
    scale = LOG2E * (width // heads) ** (-0.5)

    ids = term_ref[7]
    least = jnp.min(ids, axis=1, keepdims=True)
    most = jnp.max(ids, axis=1, keepdims=True)
    weight = jnp.left_shift(1, iota((blocks, 1), 0)).astype(F32)
    q_ids = mine_ref[rows : rows + EXTRA, 0:rows].astype(F32)[4:5, :]
    lane = iota((1, rows), 1) // SPAN
    count = jnp.int32(0)
    for s in range(spans):
        q_least = jnp.min(jnp.where(lane == s, q_ids, 1e9), axis=1, keepdims=True)
        q_most = jnp.max(jnp.where(lane == s, q_ids, -1e9), axis=1, keepdims=True)
        live = (least <= q_most) & (most >= q_least)
        bits = jnp.sum(jnp.where(live, weight, 0.0)).astype(jnp.int32)
        for place in range(blocks):
            bit = lax.bitwise_and(lax.shift_right_logical(bits, place), 1)
            table_ref[count] = jnp.int32(16 * s + place)
            count = count + bit

            @pl.when(bit == 0)
            def blank(place=place, s=s):
                s_ref[place, s] = jnp.full((SPAN * heads, LANES), -1e30, F32)

    f_ref[96:128, :] = jnp.ones((32, groups * LANES), BF16)

    def features(s, j):
        k = [term_ref[t, pl.ds(j, 1), :] for t in range(7)]
        for g in range(groups):
            at = pl.multiple_of(s * SPAN + 8 * g, 8)
            q = [qt_ref[t, pl.ds(at, 8), :] for t in range(7)]
            gap = q[1] - k[1]
            cos_gap = q[2] * k[2] + q[3] * k[3]
            dist = gap * gap + (2.0 - cos_gap)
            low = jnp.minimum(q[0], k[0])
            pair_mass = (q[6] + k[6]) + (q[4] * k[5] + q[5] * k[4] - (q[0] * k[0]) * cos_gap)
            ab = jnp.concatenate([jnp.log2(1.0 + dist), jnp.log2(1.0 + low * low * dist)], axis=0)
            cd = jnp.concatenate([low / (q[0] + k[0]), jnp.log2(pair_mass)], axis=0)
            ab_hi, ab_lo = split(ab)
            cd_hi, cd_lo = split(cd)
            f_ref[0:96, g * LANES : (g + 1) * LANES] = jnp.concatenate(
                [ab_hi, cd_hi, ab_lo, cd_lo, ab_hi, cd_hi], axis=0
            )

    def score(s, j):
        bias2 = jnp.dot(second_ref[...], act_ref[...], preferred_element_type=F32)
        bias = bias2[0:lines, :] + bias2[lines:, :]
        match = lax.dot_general(
            qm_ref[s], k_ref[j], (((1,), (1,)), ((), ())), preferred_element_type=F32
        )
        key_ids = term_ref[7, pl.ds(j, 1), :]
        for g in range(groups):
            at = pl.multiple_of(s * SPAN + 8 * g, 8)
            live = qt_ref[7, pl.ds(at, 8), :] == key_ids
            for h in range(heads):
                line = g * lines + 8 * h
                value = match[line : line + 8, :] * scale + bias[8 * h : 8 * h + 8, g * LANES : (g + 1) * LANES]
                s_ref[j, s, line : line + 8, :] = jnp.where(live, value, -1e30)

    def task(at):
        code = table_ref[jnp.clip(at, 0, count - 1)]
        return lax.shift_right_logical(code, 4), lax.bitwise_and(code, 15)

    def step(at, carry):
        hidden = jnp.dot(first_ref[...], f_ref[...], preferred_element_type=F32)
        features(*task(at + 1))
        score(*task(at - 1))
        act = hidden * (1.0 + jnp.tanh(hidden * (hidden * hidden + BETA)))
        act_ref[...] = act.astype(BF16)
        return carry

    @pl.when(count > 0)
    def run():
        features(*task(0))
        lax.fori_loop(0, count, step, 0)
        score(*task(count - 1))


def own_kernel(mine_ref, wq_ref, wk_ref, wv_ref, first_ref, second_ref, s_ref, v_ref, qt_ref, qm_ref, *scratch, heads):
    x_ref, k_ref, raw_ref, term_ref, f_ref, act_ref, table_ref = scratch
    key_side([mine_ref], [None], wk_ref, wv_ref, x_ref, k_ref, v_ref, raw_ref, term_ref)
    query_side(mine_ref, wq_ref, term_ref, qt_ref, qm_ref, heads)
    pair_scores(
        mine_ref, first_ref, second_ref, qt_ref, qm_ref, k_ref, term_ref, f_ref, act_ref, s_ref, table_ref, heads
    )


def reaches(place, flip, blocks):
    return abs(place - (place ^ flip)) <= blocks // 2


def useful(flip, blocks):
    if not skips(flip, blocks):
        return None
    own = lax.axis_index("blk")
    return jnp.abs(own - lax.bitwise_xor(own, flip)) <= blocks // 2


def skips(flip, blocks):
    return blocks == 8 and not all(reaches(place, flip, blocks) for place in range(blocks))


def near_kernel(mine_ref, *refs, flips, blocks, heads):
    count = len(flips)
    got = refs[:count]
    wk_ref, wv_ref, first_ref, second_ref, qt_ref, qm_ref, s_ref, v_ref = refs[count : count + 8]
    x_ref, k_ref, raw_ref, term_ref, f_ref, act_ref, table_ref = refs[count + 8 :]
    checks = [useful(flip, blocks) for flip in flips]
    key_side(got, checks, wk_ref, wv_ref, x_ref, k_ref, v_ref, raw_ref, term_ref)
    pair_scores(
        mine_ref, first_ref, second_ref, qt_ref, qm_ref, k_ref, term_ref, f_ref, act_ref, s_ref, table_ref, heads
    )


def last_kernel(mine_ref, *refs, flips, blocks, heads):
    count = len(flips)
    got = refs[:count]
    wk_ref, wv_ref, first_ref, second_ref, qt_ref, qm_ref = refs[count : count + 6]
    s_own, s_near, v_own, v_near, wo_ref, gain_ref, out_ref = refs[count + 6 : count + 13]
    x_ref, k_ref, raw_ref, term_ref, f_ref, act_ref, table_ref, s_ref, v_ref, att_ref = refs[count + 13 :]
    checks = [useful(flip, blocks) for flip in flips]
    key_side(got, checks, wk_ref, wv_ref, x_ref, k_ref, v_ref, raw_ref, term_ref)
    pair_scores(
        mine_ref, first_ref, second_ref, qt_ref, qm_ref, k_ref, term_ref, f_ref, act_ref, s_ref, table_ref, heads
    )
    rows = out_ref.shape[0]
    width = out_ref.shape[1]
    lines = 8 * heads
    deep = (SPAN * heads, width)
    diag = (iota(deep, 0) % lines) // 8 == iota(deep, 1) // (width // heads)
    parts = [(s_own, v_own), (s_near, v_near), (s_ref, v_ref)]

    def attend(s, carry):
        top = None
        for scores, _ in parts:
            for j in range(scores.shape[0]):
                top = scores[j, s] if top is None else jnp.maximum(top, scores[j, s])
        top = jnp.max(top, axis=1, keepdims=True)
        total = jnp.zeros((SPAN * heads, LANES), F32)
        accum = jnp.zeros(deep, F32)
        for scores, values in parts:
            pieces = []
            for j in range(scores.shape[0]):
                weights = jnp.exp2(scores[j, s] - top)
                total = total + weights
                pieces.append(weights.astype(BF16))
            accum = accum + jnp.dot(
                jnp.concatenate(pieces, axis=1),
                values[...].reshape(len(pieces) * rows, width),
                preferred_element_type=F32,
            )
        total = jnp.sum(total, axis=1, keepdims=True)
        accum = jnp.where(diag, accum / total, 0.0)
        for g in range(SPAN // 8):
            out = accum[g * lines : g * lines + 8, :]
            for h in range(1, heads):
                out = out + accum[g * lines + 8 * h : g * lines + 8 * h + 8, :]
            att_ref[pl.ds(pl.multiple_of(s * SPAN + 8 * g, 8), 8), :] = out
        return carry

    lax.fori_loop(0, rows // SPAN, attend, 0)
    mixed = jnp.dot(att_ref[...].astype(BF16), wo_ref[...], preferred_element_type=F32)
    out_ref[...] = layer_norm(mixed, gain_ref[...]).astype(BF16)


def shards(
    raw,
    raw_kin,
    reader,
    event_id,
    pre_gain,
    w_query,
    w_key,
    w_value,
    w_out,
    post_gain,
    pair_w1,
    pair_b1,
    pair_w2,
):
    groups = raw.shape[1]
    rows = raw.shape[2]
    width = raw.shape[3]
    blocks = lax.axis_size("blk")
    heads = pair_w2.shape[1]
    hidden = pair_w1.shape[1]
    assert rows == LANES and blocks & (blocks - 1) == 0 and blocks <= 32
    raw = raw[0]
    raw_kin = raw_kin[0]
    array = jax.ShapeDtypeStruct
    message = array((rows + EXTRA, width), BF16)
    vmem = pl.BlockSpec(memory_space=pltpu.VMEM)
    hbm = pl.BlockSpec(memory_space=pltpu.HBM)

    def call(kernel, out_shape, operands, scratch=(), limit=8, specs=None):
        single = not isinstance(out_shape, list)
        return pl.pallas_call(
            kernel,
            out_shape=out_shape,
            in_specs=specs or [vmem] * len(operands),
            out_specs=vmem if single else [vmem] * len(out_shape),
            scratch_shapes=list(scratch),
            compiler_params=pltpu.CompilerParams(vmem_limit_bytes=limit * MIB),
        )(*[pltpu.with_memory_space_constraint(a, pltpu.HBM) for a in operands] if specs else operands)

    small = [reader, event_id, pre_gain[None], post_gain[None]]
    packed = call(
        pack_kernel,
        [message] * groups + [array(a.shape, a.dtype) for a in small],
        [raw, raw_kin, *small],
        [pltpu.VMEM(raw_kin.shape, BF16), pltpu.SemaphoreType.DMA((groups + 5,))],
        specs=[hbm] * 6,
    )
    reader, event_id, pre_row, post_row = packed[groups:]
    parts = [packed[0]] + [
        lax.ppermute(packed[s], "grp", [(i, (i + s) % groups) for i in range(groups)])
        for s in range(1, groups)
    ]
    local = [pair_w1, pair_b1[None], pair_w2.T]
    dense = [w_query, w_key, w_value, w_out]
    w_query, w_key, w_value, w_out, first, second = call(
        weights_kernel,
        [array(a.shape, a.dtype) for a in dense]
        + [array((8 * hidden, LANES), BF16), array((16 * heads, 8 * hidden), BF16)],
        local + dense,
        [pltpu.VMEM(a.shape, a.dtype) for a in local] + [pltpu.SemaphoreType.DMA((7,))],
        specs=[hbm] * 7,
    )
    mine = call(choose_kernel, message, [reader, event_id, pre_row, first, *parts])

    along = [4, 2, 6] if blocks == 8 else list(range(2, blocks, 2))
    soon = along[:2] + [1] + along[2:]
    late = [flip ^ 1 for flip in (2, 6, 4)] if blocks == 8 else [flip ^ 1 for flip in along]

    def swap(part, flip):
        pairs = [(i, i ^ flip) for i in range(blocks)]
        if flip in along and skips(flip, blocks):
            pairs = [(i, i ^ flip if reaches(i, flip, blocks) else i ^ 1) for i in range(blocks)]
        return lax.ppermute(part, "blk", pairs)

    messages = {flip: swap(mine, flip) for flip in (soon if blocks == 8 else soon[:2])}

    spans = rows // SPAN
    lanes = SPAN // 8 * LANES
    tall = SPAN * heads

    def scratch(count):
        return [
            pltpu.VMEM((count, rows, width), BF16),
            pltpu.VMEM((count, rows, width), BF16),
            pltpu.VMEM((5, count, rows), F32),
            pltpu.VMEM((8, count, rows), F32),
            pltpu.VMEM((LANES, lanes), BF16),
            pltpu.VMEM((8 * hidden, lanes), BF16),
            pltpu.SMEM((spans * count + 1,), jnp.int32),
        ]

    def results(count):
        return [array((count, spans, tall, LANES), F32), array((count, rows, width), BF16)]

    s_own, v_own, q_terms, q_heads = call(
        lambda *refs: own_kernel(*refs, heads=heads),
        results(1) + [array((8, rows, LANES), F32), array((spans, tall, width), BF16)],
        [mine, w_query, w_key, w_value, first, second],
        scratch(1),
        limit=10,
    )
    held, q_terms = lax.optimization_barrier((mine, q_terms))
    messages.update({flip: swap(held, flip) for flip in soon if flip not in messages})
    messages.update({flip: swap(messages[flip ^ 1], 1) for flip in late})
    s_near, v_near = call(
        lambda *refs: near_kernel(*refs, flips=soon, blocks=blocks, heads=heads),
        results(len(soon)),
        [mine, *[messages[flip] for flip in soon], w_key, w_value, first, second, q_terms, q_heads],
        scratch(len(soon)),
        limit=12 + blocks // 2,
    )
    far_scratch = scratch(len(late))
    far_shapes = [
        pltpu.VMEM((len(late), spans, tall, LANES), F32),
        pltpu.VMEM((len(late), rows, width), BF16),
        pltpu.VMEM((rows, width), F32),
    ]
    encoded = call(
        lambda *refs: last_kernel(*refs, flips=late, blocks=blocks, heads=heads),
        array((rows, width), BF16),
        [mine, *[messages[flip] for flip in late], w_key, w_value, first, second, q_terms, q_heads]
        + [s_own, s_near, v_own, v_near, w_out, post_row],
        far_scratch + far_shapes,
        limit=14 + 3 * blocks // 2,
    )
    return encoded[None]


def solution(mesh):
    in_specs = (
        P("grp", None, "blk", None),
        P("grp", None, None, "blk"),
        P("grp", "blk"),
        P("grp", "blk"),
        P(),
        P(),
        P(),
        P(),
        P(),
        P(),
        P(),
        P(),
        P(),
    )
    out_specs = P("grp", "blk", None)

    return jax.shard_map(shards, mesh=mesh, in_specs=in_specs, out_specs=out_specs, check_vma=False)
```

```python
import math

import jax
import jax.numpy as jnp
from jax import lax
from jax.experimental import pallas as pl
from jax.experimental.pallas import tpu as pltpu
from jax.sharding import PartitionSpec as P


F32 = jnp.float32
BF16 = jnp.bfloat16
EXTRA = 8
LANES = 128
SPAN = 32
MIB = 1 << 20

SQ = math.sqrt(2.0 / math.pi)
GAMMA = (SQ * 0.044715) ** (1.0 / 3.0)
BETA = SQ / GAMMA
LOG2E = math.log2(math.e)
LN2 = math.log(2.0)


def iota(shape, axis):
    return lax.broadcasted_iota(jnp.int32, shape, axis)


def layer_norm(rows, gain):
    center = rows - jnp.mean(rows, axis=-1, keepdims=True)
    spread = jnp.mean(center * center, axis=-1, keepdims=True)
    return center * lax.rsqrt(spread + 1e-05) * gain


def pack_kernel(raw_ref, kin_ref, reader_ref, ids_ref, pre_ref, post_ref, *refs):
    groups, rows, width = raw_ref.shape
    messages = refs[:groups]
    copies = refs[groups : groups + 4]
    kin_own, sems = refs[groups + 4 :]
    own = lax.axis_index("grp")
    moves = [
        pltpu.make_async_copy(raw_ref.at[lax.rem(own + step, groups)], out.at[pl.ds(0, rows)], sems.at[step])
        for step, out in enumerate(messages)
    ]
    first = pltpu.make_async_copy(kin_ref, kin_own, sems.at[groups])
    first.start()
    for move in moves:
        move.start()
    others = [
        pltpu.make_async_copy(source, out, sems.at[groups + 1 + at])
        for at, (source, out) in enumerate(zip((reader_ref, ids_ref, pre_ref, post_ref), copies))
    ]
    for move in others:
        move.start()
    first.wait()
    for step, out in enumerate(messages):
        kin = kin_own[lax.rem(own + step, groups)]
        out[rows : rows + EXTRA, :] = jnp.concatenate(
            [
                jnp.concatenate([kin, jnp.zeros((4, width - rows), BF16)], axis=1),
                jnp.zeros((EXTRA - 4, width), BF16),
            ],
            axis=0,
        )
    for move in moves + others:
        move.wait()


def choose_kernel(reader_ref, ids_ref, gain_ref, ready_ref, *refs):
    got = refs[:-1]
    out = refs[-1]
    groups = len(got)
    rows = got[0].shape[0] - EXTRA
    width = got[0].shape[1]
    own = lax.axis_index("grp")
    by_lane = reader_ref[...].astype(F32)
    by_row = jnp.transpose(jnp.broadcast_to(by_lane, (LANES, rows)))
    by_row = jnp.concatenate([by_row] * (width // LANES), axis=1)
    tokens = jnp.zeros((rows, width), F32)
    kin = jnp.zeros((4, rows), F32)
    for step, ref in enumerate(got):
        source = lax.rem(own + groups - step, groups).astype(F32)
        tokens = jnp.where(by_row == source, ref[0:rows, :].astype(F32), tokens)
        kin = jnp.where(by_lane == source, ref[rows : rows + EXTRA, 0:rows].astype(F32)[0:4], kin)
    out[0:rows, :] = layer_norm(tokens, gain_ref[...]).astype(BF16)
    block = jnp.concatenate([kin, ids_ref[...].astype(F32), jnp.zeros((EXTRA - 5, rows), F32)], axis=0)
    block = jnp.concatenate([block, jnp.zeros((EXTRA, width - rows), F32)], axis=1)
    out[rows : rows + EXTRA, :] = block.astype(BF16)


def split(value):
    high = value.astype(BF16)
    return high, (value - high.astype(F32)).astype(BF16)


def weights_kernel(*refs):
    sources = refs[:7]
    copies = refs[7:11]
    first_ref, second_ref, w1_ref, b1_ref, w2_ref, sems = refs[11:]
    moves = [
        pltpu.make_async_copy(source, out, sems.at[at])
        for at, (source, out) in enumerate(zip(sources, (w1_ref, b1_ref, w2_ref, *copies)))
    ]
    for move in moves:
        move.start()
    for move in moves[:3]:
        move.wait()
    hidden = w1_ref.shape[1]
    heads = w2_ref.shape[0]
    row = lax.broadcasted_iota(jnp.int32, (4, hidden), 0)
    w1 = w1_ref[...] * jnp.where(row == 2, GAMMA, GAMMA * LN2)
    w1_hi, w1_lo = split(w1)
    b1 = b1_ref[...] * GAMMA
    b_hi, b_mid = split(b1)
    b_lo = b1 - b_hi.astype(F32) - b_mid.astype(F32)
    stack = jnp.concatenate(
        [
            w1_hi.astype(F32),
            w1_lo.astype(F32),
            b_hi.astype(F32),
            b_mid.astype(F32),
            b_lo,
            jnp.zeros((5, hidden), F32),
        ],
        axis=0,
    ).astype(BF16)

    def onehot(hit):
        return jnp.where(hit, 1.0, 0.0).astype(BF16)

    units = hidden * 8
    grown = onehot(iota((hidden, units), 1) // 8 == iota((hidden, units), 0))
    tall = jnp.dot(stack, grown, preferred_element_type=F32).astype(BF16)
    col = iota((16, LANES), 1)
    which = jnp.where(col < 32, col // 8, jnp.where(col < 96, col // 8 - 4, col - 88))
    pick = onehot((which == iota((16, LANES), 0)) & (col < 99))
    first = lax.dot_general(tall, pick, (((0,), (0,)), ((), ())), preferred_element_type=F32)
    col = iota((units, LANES), 1)
    same = (iota((units, LANES), 0) % 8 == col % 8) | (col >= 96)
    first_ref[...] = jnp.where(same, first, 0.0).astype(BF16)

    w2_hi, w2_lo = split(w2_ref[...] * (LOG2E * 0.5 / GAMMA))
    wide = [jnp.dot(w, grown, preferred_element_type=F32) for w in (w2_hi, w2_lo)]
    wide = jnp.concatenate(wide, axis=0).astype(BF16)
    shape = (16 * heads, 2 * heads)
    lift = onehot(iota(shape, 0) // 8 == iota(shape, 1))
    second = jnp.dot(lift, wide, preferred_element_type=F32)
    shape = (16 * heads, units)
    second_ref[...] = jnp.where(iota(shape, 0) % 8 == iota(shape, 1) % 8, second, 0.0).astype(BF16)
    for move in moves[3:]:
        move.wait()


def key_side(got, checks, wk_ref, wv_ref, x_ref, k_ref, v_ref, raw_ref, term_ref):
    count = len(got)
    rows = got[0].shape[0] - EXTRA
    width = got[0].shape[1]
    for place, (ref, check) in enumerate(zip(got, checks)):
        x_ref[place] = ref[0:rows, :]
        extra = ref[rows : rows + EXTRA, 0:rows].astype(F32)
        for row in range(4):
            raw_ref[row, place : place + 1, :] = extra[row : row + 1, :]
        event = extra[4:5, :]
        raw_ref[4, place : place + 1, :] = event if check is None else jnp.where(check, event, -1.0)
    feats = x_ref[...].reshape(count * rows, width)
    shape = (count, rows, width)
    k_ref[...] = jnp.dot(feats, wk_ref[...], preferred_element_type=F32).astype(BF16).reshape(shape)
    v_ref[...] = jnp.dot(feats, wv_ref[...], preferred_element_type=F32).astype(BF16).reshape(shape)
    pt = raw_ref[0]
    rap = raw_ref[1]
    phi = raw_ref[2]
    mass = raw_ref[3]
    m2 = mass * mass
    mt = jnp.sqrt(pt * pt + m2)
    terms = (pt, rap, jnp.cos(phi), jnp.sin(phi), mt * jnp.exp(rap), mt * jnp.exp(-rap), m2, raw_ref[4])
    for t, term in enumerate(terms):
        term_ref[t] = term


def query_side(mine_ref, wq_ref, term_ref, qt_ref, qm_ref, heads):
    rows = mine_ref.shape[0] - EXTRA
    width = mine_ref.shape[1]
    groups = SPAN // 8
    lines = 8 * heads
    mine = jnp.concatenate([term_ref[t, 0:1, :] for t in range(8)], axis=0)
    factor = iota((8, rows), 0)
    scaled = jnp.where((factor == 2) | (factor == 3), mine * 2.0, mine)
    scaled = jnp.where(factor == 6, mine + 1.0, scaled)
    cols = jnp.transpose(jnp.concatenate([scaled, jnp.zeros((LANES - 8, rows), F32)], axis=0))
    for t in range(8):
        qt_ref[t] = jnp.broadcast_to(cols[:, t : t + 1], (rows, LANES))
    queries = jnp.dot(mine_ref[0:rows, :], wq_ref[...], preferred_element_type=F32).astype(BF16).astype(F32)
    lane_head = iota((8, width), 1) // (width // heads)
    for g in range(rows // 8):
        piece = queries[8 * g : 8 * g + 8, :]
        qm_ref[g // groups, (g % groups) * lines : (g % groups + 1) * lines, :] = jnp.concatenate(
            [jnp.where(lane_head == h, piece, 0.0) for h in range(heads)], axis=0
        ).astype(BF16)


def pair_scores(
    mine_ref, first_ref, second_ref, qt_ref, qm_ref, k_ref, term_ref, f_ref, h_ref, act_ref, s_ref, table_ref, heads
):
    blocks, rows, width = k_ref.shape
    spans = rows // SPAN
    groups = SPAN // 8
    lines = 8 * heads
    scale = LOG2E * (width // heads) ** (-0.5)

    ids = term_ref[7]
    least = jnp.min(ids, axis=1, keepdims=True)
    most = jnp.max(ids, axis=1, keepdims=True)
    weight = jnp.left_shift(1, iota((blocks, 1), 0)).astype(F32)
    q_ids = mine_ref[rows : rows + EXTRA, 0:rows].astype(F32)[4:5, :]
    inside = iota((8, rows), 1) // SPAN == iota((8, rows), 0)
    q_least = jnp.min(jnp.where(inside, q_ids, 1e9), axis=1, keepdims=True)
    q_most = jnp.max(jnp.where(inside, q_ids, -1e9), axis=1, keepdims=True)
    joint = max(1, 24 // blocks)
    codes = []
    for base in range(0, spans, joint):
        code = jnp.zeros((blocks, 1), F32)
        for s in range(base, min(base + joint, spans)):
            live = (least <= q_most[s : s + 1]) & (most >= q_least[s : s + 1])
            code = code + jnp.where(live, weight * float(1 << (blocks * (s - base))), 0.0)
        codes.append(jnp.sum(code).astype(jnp.int32))
    count = jnp.int32(0)
    dead = jnp.int32(0)
    for s in range(spans):
        for place in range(blocks):
            bit = lax.bitwise_and(lax.shift_right_logical(codes[s // joint], blocks * (s % joint) + place), 1)
            table_ref[0, count] = jnp.int32(16 * s + place)
            table_ref[1, dead] = jnp.int32(16 * s + place)
            count = count + bit
            dead = dead + (1 - bit)

    def blank(at, carry):
        code = table_ref[1, at]
        s_ref[lax.bitwise_and(code, 15), lax.shift_right_logical(code, 4)] = jnp.full(
            (SPAN * heads, LANES), -1e30, F32
        )
        return carry

    lax.fori_loop(0, dead, blank, 0)
    f_ref[96:128, :] = jnp.ones((32, groups * LANES), BF16)

    def features(s, j):
        k = [term_ref[t, pl.ds(j, 1), :] for t in range(7)]
        for g in range(groups):
            at = pl.multiple_of(s * SPAN + 8 * g, 8)
            q = [qt_ref[t, pl.ds(at, 8), :] for t in range(7)]
            gap = q[1] - k[1]
            cos_gap = q[2] * k[2] + q[3] * k[3]
            dist = gap * gap + (2.0 - cos_gap)
            low = jnp.minimum(q[0], k[0])
            pair_mass = (q[6] + k[6]) + (q[4] * k[5] + q[5] * k[4] - (q[0] * k[0]) * cos_gap)
            ab = jnp.concatenate([jnp.log2(1.0 + dist), jnp.log2(1.0 + low * low * dist)], axis=0)
            cd = jnp.concatenate([low / (q[0] + k[0]), jnp.log2(pair_mass)], axis=0)
            ab_hi, ab_lo = split(ab)
            cd_hi, cd_lo = split(cd)
            f_ref[0:96, g * LANES : (g + 1) * LANES] = jnp.concatenate(
                [ab_hi, cd_hi, ab_lo, cd_lo, ab_hi, cd_hi], axis=0
            )

    def score(s, j):
        bias2 = jnp.dot(second_ref[...], act_ref[...], preferred_element_type=F32)
        bias = bias2[0:lines, :] + bias2[lines:, :]
        match = lax.dot_general(
            qm_ref[s], k_ref[j], (((1,), (1,)), ((), ())), preferred_element_type=F32
        )
        key_ids = term_ref[7, pl.ds(j, 1), :]
        for g in range(groups):
            at = pl.multiple_of(s * SPAN + 8 * g, 8)
            live = qt_ref[7, pl.ds(at, 8), :] == key_ids
            for h in range(heads):
                line = g * lines + 8 * h
                value = match[line : line + 8, :] * scale + bias[8 * h : 8 * h + 8, g * LANES : (g + 1) * LANES]
                s_ref[j, s, line : line + 8, :] = jnp.where(live, value, -1e30)

    def task(at):
        code = table_ref[0, jnp.clip(at, 0, count - 1)]
        return lax.shift_right_logical(code, 4), lax.bitwise_and(code, 15)

    half = groups * LANES // 2

    def activate(hidden):
        return (hidden * (1.0 + jnp.tanh(hidden * (hidden * hidden + BETA)))).astype(BF16)

    def step(at, carry):
        left = jnp.dot(first_ref[...], f_ref[:, 0:half], preferred_element_type=F32)
        right = jnp.dot(first_ref[...], f_ref[:, half:], preferred_element_type=F32)
        act_ref[:, half:] = activate(h_ref[...])
        features(*task(at + 1))
        score(*task(at - 1))
        h_ref[...] = right
        act_ref[:, 0:half] = activate(left)
        return carry

    @pl.when(count > 0)
    def run():
        features(*task(0))
        lax.fori_loop(0, count, step, 0)
        act_ref[:, half:] = activate(h_ref[...])
        score(*task(count - 1))


def own_kernel(mine_ref, wq_ref, wk_ref, wv_ref, first_ref, second_ref, s_ref, v_ref, qt_ref, qm_ref, *scratch, heads):
    x_ref, k_ref, raw_ref, term_ref, f_ref, h_ref, act_ref, table_ref = scratch
    key_side([mine_ref], [None], wk_ref, wv_ref, x_ref, k_ref, v_ref, raw_ref, term_ref)
    query_side(mine_ref, wq_ref, term_ref, qt_ref, qm_ref, heads)
    pair_scores(
        mine_ref, first_ref, second_ref, qt_ref, qm_ref, k_ref, term_ref, f_ref, h_ref, act_ref, s_ref, table_ref, heads
    )


def reaches(place, flip, blocks):
    return abs(place - (place ^ flip)) <= blocks // 2


def useful(flip, blocks):
    if not skips(flip, blocks):
        return None
    own = lax.axis_index("blk")
    return jnp.abs(own - lax.bitwise_xor(own, flip)) <= blocks // 2


def skips(flip, blocks):
    return blocks == 8 and not all(reaches(place, flip, blocks) for place in range(blocks))


def near_kernel(mine_ref, *refs, flips, blocks, heads):
    count = len(flips)
    got = refs[:count]
    wk_ref, wv_ref, first_ref, second_ref, qt_ref, qm_ref, s_ref, v_ref = refs[count : count + 8]
    x_ref, k_ref, raw_ref, term_ref, f_ref, h_ref, act_ref, table_ref = refs[count + 8 :]
    checks = [useful(flip, blocks) for flip in flips]
    key_side(got, checks, wk_ref, wv_ref, x_ref, k_ref, v_ref, raw_ref, term_ref)
    pair_scores(
        mine_ref, first_ref, second_ref, qt_ref, qm_ref, k_ref, term_ref, f_ref, h_ref, act_ref, s_ref, table_ref, heads
    )


def last_kernel(mine_ref, *refs, flips, blocks, heads):
    count = len(flips)
    got = refs[:count]
    wk_ref, wv_ref, first_ref, second_ref, qt_ref, qm_ref = refs[count : count + 6]
    s_own, s_near, v_own, v_near, wo_ref, gain_ref, out_ref = refs[count + 6 : count + 13]
    x_ref, k_ref, raw_ref, term_ref, f_ref, h_ref, act_ref, table_ref, s_ref, v_ref, att_ref, top_ref = refs[count + 13 :]
    checks = [useful(flip, blocks) for flip in flips]
    key_side(got, checks, wk_ref, wv_ref, x_ref, k_ref, v_ref, raw_ref, term_ref)
    pair_scores(
        mine_ref, first_ref, second_ref, qt_ref, qm_ref, k_ref, term_ref, f_ref, h_ref, act_ref, s_ref, table_ref, heads
    )
    rows = out_ref.shape[0]
    width = out_ref.shape[1]
    lines = 8 * heads
    deep = (SPAN * heads, width)
    diag = (iota(deep, 0) % lines) // 8 == iota(deep, 1) // (width // heads)
    parts = [(s_own, v_own), (s_near, v_near), (s_ref, v_ref)]

    def largest(s):
        top = None
        for scores, _ in parts:
            for j in range(scores.shape[0]):
                top = scores[j, s] if top is None else jnp.maximum(top, scores[j, s])
        top_ref[s] = jnp.broadcast_to(jnp.max(top, axis=1, keepdims=True), (SPAN * heads, LANES))

    def attend(s, carry):
        top = top_ref[s]
        total = jnp.zeros((SPAN * heads, LANES), F32)
        accum = jnp.zeros(deep, F32)
        for scores, values in parts:
            pieces = []
            for j in range(scores.shape[0]):
                weights = jnp.exp2(scores[j, s] - top)
                total = total + weights
                pieces.append(weights.astype(BF16))
            accum = accum + jnp.dot(
                jnp.concatenate(pieces, axis=1),
                values[...].reshape(len(pieces) * rows, width),
                preferred_element_type=F32,
            )
        largest(jnp.minimum(s + 1, rows // SPAN - 1))
        inverse = 1.0 / jnp.sum(total, axis=1, keepdims=True)
        accum = jnp.where(diag, accum * inverse, 0.0)
        for g in range(SPAN // 8):
            out = accum[g * lines : g * lines + 8, :]
            for h in range(1, heads):
                out = out + accum[g * lines + 8 * h : g * lines + 8 * h + 8, :]
            att_ref[pl.ds(pl.multiple_of(s * SPAN + 8 * g, 8), 8), :] = out
        return carry

    largest(0)
    lax.fori_loop(0, rows // SPAN, attend, 0)
    mixed = jnp.dot(att_ref[...].astype(BF16), wo_ref[...], preferred_element_type=F32)
    out_ref[...] = layer_norm(mixed, gain_ref[...]).astype(BF16)


def shards(
    raw,
    raw_kin,
    reader,
    event_id,
    pre_gain,
    w_query,
    w_key,
    w_value,
    w_out,
    post_gain,
    pair_w1,
    pair_b1,
    pair_w2,
):
    groups = raw.shape[1]
    rows = raw.shape[2]
    width = raw.shape[3]
    blocks = lax.axis_size("blk")
    heads = pair_w2.shape[1]
    hidden = pair_w1.shape[1]
    assert rows == LANES and blocks & (blocks - 1) == 0 and blocks <= 32
    raw = raw[0]
    raw_kin = raw_kin[0]
    array = jax.ShapeDtypeStruct
    message = array((rows + EXTRA, width), BF16)
    vmem = pl.BlockSpec(memory_space=pltpu.VMEM)
    hbm = pl.BlockSpec(memory_space=pltpu.HBM)

    def call(kernel, out_shape, operands, scratch=(), limit=8, specs=None):
        single = not isinstance(out_shape, list)
        return pl.pallas_call(
            kernel,
            out_shape=out_shape,
            in_specs=specs or [vmem] * len(operands),
            out_specs=vmem if single else [vmem] * len(out_shape),
            scratch_shapes=list(scratch),
            compiler_params=pltpu.CompilerParams(vmem_limit_bytes=limit * MIB),
        )(*[pltpu.with_memory_space_constraint(a, pltpu.HBM) for a in operands] if specs else operands)

    small = [reader, event_id, pre_gain[None], post_gain[None]]
    packed = call(
        pack_kernel,
        [message] * groups + [array(a.shape, a.dtype) for a in small],
        [raw, raw_kin, *small],
        [pltpu.VMEM(raw_kin.shape, BF16), pltpu.SemaphoreType.DMA((groups + 5,))],
        specs=[hbm] * 6,
    )
    reader, event_id, pre_row, post_row = packed[groups:]
    parts = [packed[0]] + [
        lax.ppermute(packed[s], "grp", [(i, (i + s) % groups) for i in range(groups)])
        for s in range(1, groups)
    ]
    local = [pair_w1, pair_b1[None], pair_w2.T]
    dense = [w_query, w_key, w_value, w_out]
    w_query, w_key, w_value, w_out, first, second = call(
        weights_kernel,
        [array(a.shape, a.dtype) for a in dense]
        + [array((8 * hidden, LANES), BF16), array((16 * heads, 8 * hidden), BF16)],
        local + dense,
        [pltpu.VMEM(a.shape, a.dtype) for a in local] + [pltpu.SemaphoreType.DMA((7,))],
        specs=[hbm] * 7,
    )
    mine = call(choose_kernel, message, [reader, event_id, pre_row, first, *parts])

    along = [4, 2, 6] if blocks == 8 else list(range(2, blocks, 2))
    soon = along[:2] + [1] + along[2:]
    late = [flip ^ 1 for flip in (2, 6, 4)] if blocks == 8 else [flip ^ 1 for flip in along]

    def swap(part, flip):
        pairs = [(i, i ^ flip) for i in range(blocks)]
        if flip in along and skips(flip, blocks):
            pairs = [(i, i ^ flip if reaches(i, flip, blocks) else i ^ 1) for i in range(blocks)]
        return lax.ppermute(part, "blk", pairs)

    messages = {flip: swap(mine, flip) for flip in (soon if blocks == 8 else soon[:2])}

    spans = rows // SPAN
    lanes = SPAN // 8 * LANES
    tall = SPAN * heads

    def scratch(count):
        return [
            pltpu.VMEM((count, rows, width), BF16),
            pltpu.VMEM((count, rows, width), BF16),
            pltpu.VMEM((5, count, rows), F32),
            pltpu.VMEM((8, count, rows), F32),
            pltpu.VMEM((LANES, lanes), BF16),
            pltpu.VMEM((8 * hidden, lanes // 2), F32),
            pltpu.VMEM((8 * hidden, lanes), BF16),
            pltpu.SMEM((2, spans * count + 1), jnp.int32),
        ]

    def results(count):
        return [array((count, spans, tall, LANES), F32), array((count, rows, width), BF16)]

    s_own, v_own, q_terms, q_heads = call(
        lambda *refs: own_kernel(*refs, heads=heads),
        results(1) + [array((8, rows, LANES), F32), array((spans, tall, width), BF16)],
        [mine, w_query, w_key, w_value, first, second],
        scratch(1),
        limit=10,
    )
    held, q_terms = lax.optimization_barrier((mine, q_terms))
    messages.update({flip: swap(held, flip) for flip in soon if flip not in messages})
    messages.update({flip: swap(messages[flip ^ 1], 1) for flip in late})
    s_near, v_near = call(
        lambda *refs: near_kernel(*refs, flips=soon, blocks=blocks, heads=heads),
        results(len(soon)),
        [mine, *[messages[flip] for flip in soon], w_key, w_value, first, second, q_terms, q_heads],
        scratch(len(soon)),
        limit=12 + blocks // 2,
    )
    far_scratch = scratch(len(late))
    far_shapes = [
        pltpu.VMEM((len(late), spans, tall, LANES), F32),
        pltpu.VMEM((len(late), rows, width), BF16),
        pltpu.VMEM((rows, width), F32),
        pltpu.VMEM((spans, tall, LANES), F32),
    ]
    encoded = call(
        lambda *refs: last_kernel(*refs, flips=late, blocks=blocks, heads=heads),
        array((rows, width), BF16),
        [mine, *[messages[flip] for flip in late], w_key, w_value, first, second, q_terms, q_heads]
        + [s_own, s_near, v_own, v_near, w_out, post_row],
        far_scratch + far_shapes,
        limit=14 + 3 * blocks // 2,
    )
    return encoded[None]


def solution(mesh):
    in_specs = (
        P("grp", None, "blk", None),
        P("grp", None, None, "blk"),
        P("grp", "blk"),
        P("grp", "blk"),
        P(),
        P(),
        P(),
        P(),
        P(),
        P(),
        P(),
        P(),
        P(),
    )
    out_specs = P("grp", "blk", None)

    return jax.shard_map(shards, mesh=mesh, in_specs=in_specs, out_specs=out_specs, check_vma=False)
```
